256 devices in a mesh: blk: 8 (over x, core), uly: 8 (over z), tp: 4 (over y).
Axes of the slice: x: 4, y: 4, z: 8, core: 2. Of those that a mesh axis runs over, the one named last changes fastest.
Arguments:
- hidden: bfloat16 [8192, 8192], P(('blk', 'uly')), may hold values from -8 to 8
- norm_gain: bfloat16 [8192], replicated, may hold values from 0.099609375 to 1.8984375
- query_key_value_weight: bfloat16 [8192, 4, 1280], P('uly', 'tp'), may hold values from -1 to 1
- w_out: bfloat16 [4096, 8192], P('tp', 'uly'), may hold values from -0.5 to 0.5
- doc_ids: int32 [8192], replicated, may hold values from 0 to 15, never falling along the last dimension, each value on 1 to 2048 neighbouring positions
- block_order: int32 [16], replicated, may hold values from 0 to 15, each once
Outputs:
- attn_out: bfloat16 [8192, 8192], P(('blk', 'tp'), 'uly')
The draws below stay inside these ranges and needn't reach their ends.
Inputs may be any that keep to these rules, and one draw needn't show every extreme that they name: `doc_ids`: never falls along the sequence; every document holds 1 to 2048 positions and one holds exactly 2048. Array rows c * 512 to (c + 1) * 512 - 1 hold sequence block block_order[c]; every block appears once.
All inputs are finite; a program needn't handle non-finite values.
Results may differ from the reference program's by a relative error of at most 0.029.
Values may be sent and summed in bfloat16 or wider, within the bound.
A program may use at most 64 MiB of HBM per device.

```python
import math
import jax
import jax.numpy as jnp
import numpy as np
from jax import lax

MODEL_WIDTH = 8192
QUERY_HEAD_COUNT = 32
KV_HEAD_COUNT = 4
HEAD_SIZE = 128
BLOCK = 512
NBLOCK = 16
PACKED_TOKENS = 8192


def draw_hidden(key, part):
    own_key = jax.random.fold_in(key, 2)
    values = jnp.clip(jax.random.normal(own_key, (PACKED_TOKENS, MODEL_WIDTH), jnp.float32), -6.0, 6.0)
    return values.astype(jnp.bfloat16)


def draw_query_key_value_weight(key, part):
    own_key = jax.random.fold_in(key, 3)
    group_width = QUERY_HEAD_COUNT // KV_HEAD_COUNT
    complete_shape = (MODEL_WIDTH, KV_HEAD_COUNT, (group_width + 2) * HEAD_SIZE)
    values = jnp.clip(jax.random.normal(own_key, complete_shape, jnp.float32), -6.0, 6.0) * MODEL_WIDTH ** (-0.5)
    return values.astype(jnp.bfloat16)


def steps_of(key, dims, shards, least, high):
    gain, own = 1.0, jax.random.fold_in(key, 6)
    for axis_at, parts in shards:
        steps = jnp.exp(jax.random.uniform(jax.random.fold_in(own, axis_at), (parts,), jnp.float32, least / len(shards), high / len(shards)))
        gain = gain * jnp.repeat(steps, dims[axis_at] // parts).reshape([-1 if axis == axis_at else 1 for axis in range(len(dims))])
    return gain


def length_profile(amount, total, most, slope):
    portions = [(1 << 20) // math.isqrt(grade ** slope) + 1 for grade in range(2, amount + 1)]
    surplus, counts = total - most - (amount - 1), [1] * (amount - 1)
    while surplus > 0:
        candidates = [i for i in range(amount - 1) if counts[i] < most]
        whole, budget = sum([portions[i] for i in candidates]), surplus
        for i in candidates:
            extra = min(most - counts[i], max(1, budget * portions[i] // whole), surplus)
            counts[i] = counts[i] + extra
            surplus = surplus - extra
    return np.array([most] + counts)


def ragged_sizes(stream_key, count, total, most, slope):
    if count == 2:
        one = jax.random.randint(stream_key, (), max(1, total - most), min(most, total - 1) + 1)
        return jnp.stack([one, total - one])
    sizes = jnp.asarray(length_profile(count, total, most, slope), jnp.int32)
    couples = (count - 1) // 2
    donor, receiver = sizes[1:1 + 2 * couples:2], sizes[2:2 + 2 * couples:2]
    slack = jnp.minimum(donor - 1, most - receiver)
    moved = jax.random.randint(jax.random.fold_in(stream_key, 1), (couples,), 0, 1 << 20) % (slack + 1)
    sizes = sizes.at[1:1 + 2 * couples:2].set(donor - moved).at[2:2 + 2 * couples:2].set(receiver + moved)
    return sizes[jax.random.permutation(jax.random.fold_in(stream_key, 2), count)]


def bell_draw(key, dims, deviation, reach, cuts=(), kind=jnp.bfloat16):
    gain = steps_of(key, dims, cuts, -0.22, 0.18) if cuts else 1.0
    result = jax.random.normal(key, dims, jnp.float32) * deviation * gain
    return jnp.minimum(jnp.maximum(result, -reach), reach).astype(kind)


def setup_inputs(seed: int = 0) -> dict:
    keys = jax.random.split(jax.random.key(seed), 7)
    hidden = draw_hidden(jax.random.fold_in(keys[6], 71), 0)
    norm_gain = jnp.clip(1.0 + 0.18 * jax.random.normal(keys[1], (MODEL_WIDTH,), jnp.float32), 0.099609375, 1.8984375).astype(jnp.bfloat16)
    query_key_value_weight = draw_query_key_value_weight(jax.random.fold_in(keys[6], 71), 0)
    w_out = bell_draw(keys[3], (QUERY_HEAD_COUNT * HEAD_SIZE, MODEL_WIDTH), HEAD_SIZE ** -0.5, 0.5, ((0, 4), (1, 8)))
    doc_ids = jnp.searchsorted(jnp.cumsum(ragged_sizes(keys[4], NBLOCK, PACKED_TOKENS, 4 * BLOCK, 1)), jnp.arange(PACKED_TOKENS), side="right").astype(jnp.int32)
    block_order = jax.random.permutation(keys[5], NBLOCK).astype(jnp.int32)
    return dict(hidden=hidden, norm_gain=norm_gain, query_key_value_weight=query_key_value_weight, w_out=w_out, doc_ids=doc_ids, block_order=block_order)


THETA = 500000.0
NEG_BIG = -1e+30

def rope_tables(positions):
    half_dim = HEAD_SIZE // 2
    lane_ids = jnp.arange(half_dim).astype(jnp.float32)
    base_freq = jnp.power(THETA, -2.0 * lane_ids / HEAD_SIZE)
    wavelen = 2.0 * math.pi / base_freq
    smooth = (8192.0 / wavelen - 1.0) / 3.0
    blended = (1.0 - smooth) * base_freq / 8.0 + smooth * base_freq
    scaled = jnp.where(wavelen > 8192.0, base_freq / 8.0, jnp.where(wavelen < 2048.0, base_freq, blended))
    angles = positions.astype(jnp.float32)[:, None] * scaled[None, :]
    return (jnp.cos(angles), jnp.sin(angles))

def rotate(values, cos_table, sin_table):
    half_dim = values.shape[-1] // 2
    leading = values[..., :half_dim]
    trailing = values[..., half_dim:]
    cos_part = cos_table[:, None, :]
    sin_part = sin_table[:, None, :]
    return jnp.concatenate([leading * cos_part - trailing * sin_part, trailing * cos_part + leading * sin_part], axis=-1)

def positions_of(block_order, row_ids):
    block_ids = row_ids // BLOCK
    matches = block_ids[:, None] == jnp.arange(block_order.shape[0]).astype(jnp.int32)[None, :]
    seq_block = lax.optimization_barrier(jnp.sum(jnp.where(matches, block_order[None, :], 0), axis=1))
    return (seq_block * BLOCK + row_ids % BLOCK).astype(jnp.int32)

def reference(hidden, norm_gain, query_key_value_weight, w_out, doc_ids, block_order):
    group_width = QUERY_HEAD_COUNT // KV_HEAD_COUNT
    widened = hidden.astype(jnp.float32)
    inverse_rms = lax.rsqrt(lax.optimization_barrier(jnp.mean(widened * widened, axis=1, keepdims=True)) + 1e-05)
    rms_scaled = (widened * inverse_rms * norm_gain.astype(jnp.float32)[None, :]).astype(jnp.bfloat16)
    projected_rows = jnp.dot(rms_scaled, query_key_value_weight.reshape(MODEL_WIDTH, KV_HEAD_COUNT * (group_width + 2) * HEAD_SIZE), preferred_element_type=jnp.float32)
    projected_rows = projected_rows.reshape(PACKED_TOKENS, KV_HEAD_COUNT, group_width + 2, HEAD_SIZE)
    row_ids = jnp.arange(PACKED_TOKENS).astype(jnp.int32)
    positions = positions_of(block_order, row_ids)
    segments = jnp.take(doc_ids, positions)
    cos_table, sin_table = rope_tables(positions)
    queries = rotate(projected_rows[:, :, :group_width, :].reshape(PACKED_TOKENS, QUERY_HEAD_COUNT, HEAD_SIZE), cos_table, sin_table).astype(jnp.bfloat16)
    keys_all = rotate(projected_rows[:, :, group_width, :], cos_table, sin_table).astype(jnp.bfloat16)
    values_all = projected_rows[:, :, group_width + 1, :].astype(jnp.bfloat16)
    query_heads = jnp.transpose(queries, (1, 0, 2))
    key_heads = jnp.transpose(keys_all, (1, 0, 2))
    value_heads = jnp.transpose(values_all, (1, 0, 2))
    block_len = 2 * BLOCK
    block_count = PACKED_TOKENS // block_len
    inv_root = 1.0 / math.sqrt(HEAD_SIZE)

    def per_head(head_id):
        query_rows = lax.dynamic_index_in_dim(query_heads, head_id, 0, keepdims=False)
        key_rows = lax.dynamic_index_in_dim(key_heads, head_id // group_width, 0, keepdims=False)
        value_rows = lax.dynamic_index_in_dim(value_heads, head_id // group_width, 0, keepdims=False)

        def per_block(block_id):
            offset = (block_id * block_len).astype(jnp.int32)
            query_blk = lax.dynamic_slice_in_dim(query_rows, offset, block_len, 0)
            query_pos = lax.dynamic_slice_in_dim(positions, offset, block_len, 0)
            query_seg = lax.dynamic_slice_in_dim(segments, offset, block_len, 0)
            scores = jnp.dot(query_blk, key_rows.T, preferred_element_type=jnp.float32) * inv_root
            allowed = (positions[None, :] <= query_pos[:, None]) & (segments[None, :] == query_seg[:, None])
            scores = jnp.where(allowed, scores, NEG_BIG)
            row_max = lax.optimization_barrier(jnp.max(scores, axis=1, keepdims=True))
            weights = jnp.where(allowed, jnp.exp(scores - row_max), 0.0)
            row_sum = lax.optimization_barrier(jnp.sum(weights, axis=1, keepdims=True))
            mixed_rows = jnp.dot(weights.astype(jnp.bfloat16), value_rows, preferred_element_type=jnp.float32)
            return (mixed_rows / row_sum).astype(jnp.bfloat16)
        return lax.map(per_block, jnp.arange(block_count).astype(jnp.int32)).reshape(PACKED_TOKENS, HEAD_SIZE)
    attended = lax.map(per_head, jnp.arange(QUERY_HEAD_COUNT).astype(jnp.int32))
    flattened = jnp.transpose(attended, (1, 0, 2)).reshape(PACKED_TOKENS, QUERY_HEAD_COUNT * HEAD_SIZE)
    return jnp.dot(flattened, w_out, preferred_element_type=jnp.float32).astype(jnp.bfloat16)
```

```python
import math

import jax
import jax.numpy as jnp
from jax import lax
from jax.experimental import pallas as pl
from jax.experimental.pallas import tpu as pltpu
from jax.sharding import PartitionSpec as P

HEAD = 128
HEADS = 8
BLOCK = 512
THETA = 500000.0
NEG_BIG = -1e30
NZ = 8
NT = 4
ROWS = 128
SUB = ROWS // NT
FEAT = 1024
COLS = (HEADS + 2) * HEAD
HALF = COLS // 2
MESH = pl.DeviceIdType.MESH
F32 = jnp.float32
BF16 = jnp.bfloat16
FAR_FIRST = (4, 3, 5, 2, 6, 1, 7)
QSCALE = math.log2(math.e) / math.sqrt(HEAD)


def remote(src, dst, send_sem, recv_sem, device):
    return pltpu.make_async_remote_copy(
        src_ref=src,
        dst_ref=dst,
        send_sem=send_sem,
        recv_sem=recv_sem,
        device_id=device,
        device_id_type=MESH,
    )


def greet(devices):
    barrier = pltpu.get_barrier_semaphore()
    for device in devices:
        pl.semaphore_signal(barrier, inc=1, device_id=device, device_id_type=MESH)
    pl.semaphore_wait(barrier, len(devices))


def dot32(a, b):
    return jnp.dot(a, b, preferred_element_type=F32)


def proj_kernel(
    hid, w, gain, cos, sin, q_out, kv_out,
    hloc, wloc, wg, xbuf, own, far, pairs, stage, inbox,
    lsem, zs, zr, ys, yr, fs, fr, rs, rr,
):
    u = lax.axis_index("uly")
    t = lax.axis_index("tp")
    t_right, t_left = lax.rem(t + 1, NT), lax.rem(t + NT - 1, NT)
    u_right, u_left = lax.rem(u + 1, NZ), lax.rem(u + NZ - 1, NZ)
    load_w = pltpu.make_async_copy(w, wloc, lsem.at[0])
    load_h = pltpu.make_async_copy(hid, hloc, lsem.at[1])
    load_w.start()
    load_h.start()
    greet(
        [{"uly": lax.rem(u + k, NZ)} for k in range(1, NZ)]
        + [{"tp": t_right}, {"tp": t_left}]
    )
    rows = pl.ds(pl.multiple_of(t * SUB, SUB), SUB)
    over_z = []
    for i, k in enumerate(FAR_FIRST):
        v = lax.rem(u + NZ - k, NZ)
        copy = remote(
            hid.at[rows, pl.ds(pl.multiple_of(v * FEAT, FEAT), FEAT)],
            xbuf.at[i, t], zs.at[i], zr.at[i], {"uly": v},
        )
        copy.start()
        over_z.append(copy)
    load_w.wait()

    def fold(c, carry):
        r = pl.ds(pl.multiple_of(c * 128, 128), 128)
        wg[r, :] = (wloc[r, :].astype(F32) * gain[r, :]).astype(BF16)
        return carry

    lax.fori_loop(0, FEAT // 128, fold, 0)
    load_h.wait()

    def square(c, acc):
        x = hloc[:, pl.ds(pl.multiple_of(c * 128, 128), 128)].astype(F32)
        return acc + x * x

    total = lax.fori_loop(0, NZ * FEAT // 128, square, jnp.zeros((ROWS, 128), F32))
    scale = lax.rsqrt(jnp.sum(total, axis=1, keepdims=True) / (NZ * FEAT) + 1e-05)
    own[...] = dot32(hloc[:, pl.ds(pl.multiple_of(u * FEAT, FEAT), FEAT)], wg[...])

    def chunk_from(i, source, direction):
        return remote(
            xbuf.at[i, source], xbuf.at[i, source], ys.at[i, direction], yr.at[i, direction],
            {"tp": t_right if direction == 0 else t_left},
        )

    def pass_on(i):
        if i % 2 == 0:
            return remote(xbuf.at[i, t_left], xbuf.at[i, t_left], fs.at[i], fr.at[i], {"tp": t_right})
        return remote(xbuf.at[i, t_right], xbuf.at[i, t_right], fs.at[i], fr.at[i], {"tp": t_left})

    def send_sum(step, direction, piece):
        return remote(
            stage.at[direction, step, piece], inbox.at[direction, step, piece],
            rs.at[direction, step, piece], rr.at[direction, step, piece],
            {"uly": u_right if direction == 0 else u_left},
        )

    def start_sum(step, direction, piece, value):
        stage[direction, step, piece] = value.astype(BF16)
        send_sum(step, direction, piece).start()

    def cols(piece):
        return slice(piece * HALF, (piece + 1) * HALF)

    count = NZ - 1
    across = lax.rem(t + 2, NT)
    for tick in range(count + 2):
        if tick < count:
            over_z[tick].wait_recv()
            chunk_from(tick, t, 0).start()
            chunk_from(tick, t, 1).start()
        i = tick - 1
        if 0 <= i < count:
            chunk_from(i, t_left, 0).wait_recv()
            chunk_from(i, t_right, 1).wait_recv()
            pass_on(i).start()
        i = tick - 2
        if 0 <= i < count:
            remote(
                xbuf.at[i, across], xbuf.at[i, across], fs.at[i], fr.at[i], {"tp": t_right}
            ).wait_recv()
            if i == 0:
                far[...] = dot32(xbuf[0].reshape(ROWS, FEAT), wg[...])
                start_sum(0, 0, 0, far[:, cols(0)])
                start_sum(0, 1, 1, far[:, cols(1)])
            elif i % 2 == 0:
                j = i // 2
                x = xbuf[i - 1 : i + 1].reshape(2 * ROWS, FEAT)
                pairs[j - 1] = dot32(x, wg[...])
                if j == 1:
                    start_sum(1, 0, 1, pairs[0, :ROWS, cols(1)])
                    start_sum(1, 1, 0, pairs[0, ROWS:, cols(0)])

    for j in range(1, 4):
        for order in range(2):
            for direction in range(2):
                piece = order if direction == 0 else 1 - order
                if j == 1 and order == 1:
                    continue
                send_sum(j - 1, direction, piece).wait_recv()
                mine = pairs[j - 1, direction * ROWS : (direction + 1) * ROWS, cols(piece)]
                start_sum(j, direction, piece, mine + inbox[direction, j - 1, piece].astype(F32))
    for direction in range(2):
        for piece in range(2):
            send_sum(3, direction, piece).wait_recv()
    for piece in range(2):
        summed = own[:, cols(piece)]
        summed = summed + inbox[0, 3, piece].astype(F32)
        summed = summed + inbox[1, 3, piece].astype(F32)
        own[:, cols(piece)] = summed * scale
    for h in range(HEADS + 1):
        x = own[:, h * HEAD : (h + 1) * HEAD]
        x = x * cos[...] + pltpu.roll(x, HEAD // 2, 1) * sin[...]
        if h < HEADS:
            q_out[h * ROWS : (h + 1) * ROWS, :] = (x * QSCALE).astype(BF16)
        else:
            kv_out[:, :HEAD] = x.astype(BF16)
    kv_out[:, HEAD:] = own[:, (HEADS + 1) * HEAD :].astype(BF16)

    for i in range(count):
        over_z[i].wait_send()
        chunk_from(i, t, 0).wait_send()
        chunk_from(i, t, 1).wait_send()
        pass_on(i).wait_send()
    for direction in range(2):
        for step in range(4):
            for piece in range(2):
                if step > 0 or piece == direction:
                    send_sum(step, direction, piece).wait_send()


ANY = pl.BlockSpec(memory_space=pl.ANY)
VM = pl.BlockSpec(memory_space=pltpu.VMEM)
DMA = pltpu.SemaphoreType.DMA


def project(hidden, weights, gain, cos, sin):
    n = NZ - 1
    return pl.pallas_call(
        proj_kernel,
        out_shape=(
            jax.ShapeDtypeStruct((HEADS * ROWS, HEAD), BF16),
            jax.ShapeDtypeStruct((ROWS, 2 * HEAD), BF16),
        ),
        in_specs=[ANY, ANY, VM, VM, VM],
        out_specs=(VM, VM),
        scratch_shapes=[
            pltpu.VMEM((ROWS, NZ * FEAT), BF16),
            pltpu.VMEM((FEAT, COLS), BF16),
            pltpu.VMEM((FEAT, COLS), BF16),
            pltpu.VMEM((n, NT, SUB, FEAT), BF16),
            pltpu.VMEM((ROWS, COLS), F32),
            pltpu.VMEM((ROWS, COLS), F32),
            pltpu.VMEM((3, 2 * ROWS, COLS), F32),
            pltpu.VMEM((2, 4, 2, ROWS, HALF), BF16),
            pltpu.VMEM((2, 4, 2, ROWS, HALF), BF16),
            DMA((2,)),
            DMA((n,)), DMA((n,)),
            DMA((n, 2)), DMA((n, 2)),
            DMA((n,)), DMA((n,)),
            DMA((2, 4, 2)), DMA((2, 4, 2)),
        ],
        compiler_params=pltpu.CompilerParams(
            collective_id=0, has_side_effects=True, vmem_limit_bytes=40 << 20
        ),
        name="project",
    )(hidden, weights, gain, cos, sin)


Z_STEPS = (0, -1, 1, -2, 2, -3, 3, -4)


def gather_kernel(kv, out, lsem, zs, zr, xs, xr, fs, fr, ss, sr):
    b = lax.axis_index("blk")
    u = lax.axis_index("uly")
    u_right, u_left = lax.rem(u + 1, NZ), lax.rem(u + NZ - 1, NZ)
    b_right, b_left, b_across = lax.rem(b + 2, 8), lax.rem(b + 6, 8), lax.rem(b + 4, 8)
    sibling = b + 1 - 2 * lax.rem(b, 2)
    own = pltpu.make_async_copy(kv, out.at[b * NZ + u], lsem)
    own.start()
    greet([{"uly": u_right}, {"uly": u_left}, {"blk": b_right}, {"blk": b_left}, {"blk": sibling}])

    def z_of(i):
        return lax.rem(u + Z_STEPS[i] + NZ, NZ)

    def shard(owner, i):
        return out.at[owner * NZ + z_of(i)]

    def z_copy(i, src, dst):
        step = Z_STEPS[i]
        return remote(src, dst, zs.at[i], zr.at[i], {"uly": u_right if step < 0 else u_left})

    def z_send(step, src_i):
        i = Z_STEPS.index(step)
        src = kv if src_i == 0 else shard(b, src_i)
        return z_copy(i, src, shard(b, src_i))

    def x_send(i, direction):
        src = kv if i == 0 else shard(b, i)
        return remote(
            src, shard(b, i), xs.at[i, direction], xr.at[i, direction],
            {"blk": b_right if direction == 0 else b_left},
        )

    def x_wait(i, direction):
        source = b_left if direction == 0 else b_right
        return remote(
            shard(source, i), shard(source, i), xs.at[i, direction], xr.at[i, direction],
            {"blk": b_right},
        )

    def pass_on(i):
        source, target = (b_left, b_right) if i % 2 == 0 else (b_right, b_left)
        return remote(shard(source, i), shard(source, i), fs.at[i], fr.at[i], {"blk": target})

    def side(i, m):
        owner = (b, b_left, b_right, b_across)[m]
        src = kv if (i == 0 and m == 0) else shard(owner, i)
        return remote(src, shard(owner, i), ss.at[i, m], sr.at[i, m], {"blk": sibling})

    def side_wait(i, m):
        off = (0, 6, 2, 4)[m]
        owner = lax.rem(sibling + off, 8)
        return remote(shard(owner, i), shard(owner, i), ss.at[i, m], sr.at[i, m], {"blk": sibling})

    z_sends = {}

    def start_z(step, src_i):
        copy = z_send(step, src_i)
        copy.start()
        z_sends[step] = copy

    for tick in range(NZ + 2):
        i = tick
        if i < NZ:
            step = Z_STEPS[i]
            if i == 0:
                start_z(-1, 0)
                start_z(1, 0)
            else:
                z_copy(i, shard(b, i), shard(b, i)).wait_recv()
                if step < 0 and step > -4:
                    start_z(step - 1, i)
                if step > 0 and step < 3:
                    start_z(step + 1, i)
            x_send(i, 0).start()
            x_send(i, 1).start()
            side(i, 0).start()
        i = tick - 1
        if 0 <= i < NZ:
            x_wait(i, 0).wait_recv()
            x_wait(i, 1).wait_recv()
            pass_on(i).start()
            side(i, 1).start()
            side(i, 2).start()
        i = tick - 2
        if 0 <= i < NZ:
            remote(
                shard(b_across, i), shard(b_across, i), fs.at[i], fr.at[i], {"blk": b_right}
            ).wait_recv()
            side(i, 3).start()
    own.wait()
    for i in range(NZ):
        for m in range(4):
            side_wait(i, m).wait_recv()
    for copy in z_sends.values():
        copy.wait_send()
    for i in range(NZ):
        x_send(i, 0).wait_send()
        x_send(i, 1).wait_send()
        pass_on(i).wait_send()
        for m in range(4):
            side(i, m).wait_send()


def gather_kv(kv):
    return pl.pallas_call(
        gather_kernel,
        out_shape=jax.ShapeDtypeStruct((8 * NZ, ROWS, 2 * HEAD), BF16),
        in_specs=[VM],
        out_specs=VM,
        scratch_shapes=[
            DMA(()),
            DMA((NZ,)), DMA((NZ,)),
            DMA((NZ, 2)), DMA((NZ, 2)),
            DMA((NZ,)), DMA((NZ,)),
            DMA((NZ, 4)), DMA((NZ, 4)),
        ],
        compiler_params=pltpu.CompilerParams(
            collective_id=1, has_side_effects=True, vmem_limit_bytes=24 << 20
        ),
        name="gather_kv",
    )(kv)


def attend_kernel(table, q, q_start, kv, out, m_ref, l_ref, acc):
    count, q_block = table[0], table[1]
    wide = HEADS * ROWS
    m_ref[...] = jnp.full((1, wide), NEG_BIG, F32)
    l_ref[...] = jnp.zeros((1, wide), F32)
    acc[...] = jnp.zeros((HEAD, wide), F32)
    lane = lax.broadcasted_iota(jnp.int32, (128, ROWS), 1)
    row = lax.broadcasted_iota(jnp.int32, (128, ROWS), 0)
    causal = row <= lane
    starts = jnp.broadcast_to(q_start[...], (128, ROWS))

    def step(i, carry):
        k_block = q_block - i
        at = table[2 + k_block]
        k = kv[at, :, :HEAD]
        v = kv[at, :, HEAD:]
        scores = lax.dot_general(
            k, q[...], (((1,), (1,)), ((), ())), preferred_element_type=F32
        )
        allowed = (row + k_block * 128 >= starts) & (causal | (i > 0))
        bias = jnp.where(allowed, 0.0, NEG_BIG)
        scores = scores + jnp.concatenate([bias] * HEADS, axis=1)
        m_old = m_ref[...]
        m_new = jnp.maximum(m_old, jnp.max(scores, axis=0, keepdims=True))
        weights = jnp.exp2(scores - m_new)
        factor = jnp.exp2(m_old - m_new)
        m_ref[...] = m_new
        l_ref[...] = l_ref[...] * factor + jnp.sum(weights, axis=0, keepdims=True)
        mixed = lax.dot_general(
            v, weights.astype(BF16), (((0,), (0,)), ((), ())), preferred_element_type=F32
        )
        acc[...] = acc[...] * factor + mixed
        return carry

    lax.fori_loop(0, count, step, 0)
    result = acc[...] / l_ref[...]
    for h in range(HEADS):
        part = result[:, h * ROWS : (h + 1) * ROWS]
        out[:, h * HEAD : (h + 1) * HEAD] = part.T.astype(BF16)


def attend(table, q, q_start, kv):
    wide = HEADS * ROWS
    return pl.pallas_call(
        attend_kernel,
        out_shape=jax.ShapeDtypeStruct((ROWS, HEADS * HEAD), BF16),
        in_specs=[pl.BlockSpec(memory_space=pltpu.SMEM), VM, VM, VM],
        out_specs=VM,
        scratch_shapes=[
            pltpu.VMEM((1, wide), F32),
            pltpu.VMEM((1, wide), F32),
            pltpu.VMEM((HEAD, wide), F32),
        ],
        compiler_params=pltpu.CompilerParams(vmem_limit_bytes=24 << 20),
        name="attend",
    )(table, q, q_start, kv)


PIECES = 2
PROWS = ROWS // PIECES
OUTW = 1024


def out_kernel(att, w, out, wloc, abuf, far_stage, near_stage, far_box, near_box,
               lsem, zs, zr, fs, fr, ns, nr):
    u = lax.axis_index("uly")
    t = lax.axis_index("tp")
    t_right, t_left = lax.rem(t + 1, NT), lax.rem(t + NT - 1, NT)
    u_right, u_left = lax.rem(u + 1, NZ), lax.rem(u + NZ - 1, NZ)
    load_w = pltpu.make_async_copy(w, wloc, lsem.at[0])
    load_w.start()
    own_copies = []
    for p in range(PIECES):
        copy = pltpu.make_async_copy(att.at[p], abuf.at[u, p], lsem.at[1 + p])
        copy.start()
        own_copies.append(copy)
    greet([{"uly": u_right}, {"uly": u_left}, {"tp": t_right}, {"tp": t_left}])

    def z_hops(p, direction):
        return 4 if (p + direction) % 2 == 0 else 3

    def chunk(direction, h):
        return lax.rem(u + NZ + (-h if direction == 0 else h), NZ)

    def z_copy(p, direction, h, source):
        src = att.at[p] if h == 0 else abuf.at[source, p]
        return remote(
            src, abuf.at[source, p], zs.at[p, direction, h], zr.at[p, direction, h],
            {"uly": u_right if direction == 0 else u_left},
        )

    def z_send(p, direction, h):
        return z_copy(p, direction, h, chunk(direction, h))

    def z_wait(p, direction, h):
        source = chunk(direction, h + 1)
        return remote(
            abuf.at[source, p], abuf.at[source, p], zs.at[p, direction, h],
            zr.at[p, direction, h], {"uly": u_right},
        )

    def z_step(p, h):
        for direction in range(2):
            hops = z_hops(p, direction)
            if h > 0 and h <= hops:
                z_wait(p, direction, h - 1).wait_recv()
            if h < hops:
                z_send(p, direction, h).start()

    def product(p, rel):
        d = lax.rem(t + rel, NT)
        x = abuf[pl.ds(2 * d, 2), p].reshape(2 * PROWS, FEAT)
        return dot32(x, wloc[...])

    def half(side):
        return slice(side * (OUTW // 2), (side + 1) * (OUTW // 2))

    def far_send(p, side):
        return remote(
            far_stage.at[p, side], far_box.at[p, side], fs.at[p, side], fr.at[p, side],
            {"tp": t_right if side == 0 else t_left},
        )

    def near_send(p, direction, side):
        return remote(
            near_stage.at[p, direction, side], near_box.at[p, direction, side],
            ns.at[p, direction, side], nr.at[p, direction, side],
            {"tp": t_right if direction == 0 else t_left},
        )

    for p in range(PIECES):
        z_step(p, 0)
    load_w.wait()
    for copy in own_copies:
        copy.wait()
    for h in range(1, 5):
        z_step(0, h)
    for p in range(PIECES):
        more = p + 1 < PIECES
        value = product(p, 2)
        for side in range(2):
            far_stage[p, side] = value[:, half(side)].astype(BF16)
            far_send(p, side).start()
        if more:
            z_step(p + 1, 1)
        right = product(p, 1)
        near_stage[p, 0, 1] = right[:, half(1)].astype(BF16)
        near_send(p, 0, 1).start()
        left = product(p, 3)
        near_stage[p, 1, 0] = left[:, half(0)].astype(BF16)
        near_send(p, 1, 0).start()
        if more:
            z_step(p + 1, 2)
        far_send(p, 0).wait_recv()
        near_stage[p, 0, 0] = (right[:, half(0)] + far_box[p, 0].astype(F32)).astype(BF16)
        near_send(p, 0, 0).start()
        far_send(p, 1).wait_recv()
        near_stage[p, 1, 1] = (left[:, half(1)] + far_box[p, 1].astype(F32)).astype(BF16)
        near_send(p, 1, 1).start()
        if more:
            z_step(p + 1, 3)
        mine = product(p, 0)
        if more:
            z_step(p + 1, 4)
        for side in range(2):
            near_send(p, 0, side).wait_recv()
            near_send(p, 1, side).wait_recv()
            summed = mine[:, half(side)] + near_box[p, 0, side].astype(F32)
            summed = summed + near_box[p, 1, side].astype(F32)
            out[:, p, :, half(side)] = summed.reshape(2, PROWS, OUTW // 2).astype(BF16)
    for p in range(PIECES):
        for direction in range(2):
            for h in range(z_hops(p, direction)):
                z_send(p, direction, h).wait_send()
            far_send(p, direction).wait_send()
            for side in range(2):
                near_send(p, direction, side).wait_send()


def project_out(attended, w):
    half = OUTW // 2
    out = pl.pallas_call(
        out_kernel,
        out_shape=jax.ShapeDtypeStruct((2, PIECES, PROWS, OUTW), BF16),
        in_specs=[ANY, ANY],
        out_specs=VM,
        scratch_shapes=[
            pltpu.VMEM((FEAT, OUTW), BF16),
            pltpu.VMEM((NZ, PIECES, PROWS, FEAT), BF16),
            pltpu.VMEM((PIECES, 2, 2 * PROWS, half), BF16),
            pltpu.VMEM((PIECES, 2, 2, 2 * PROWS, half), BF16),
            pltpu.VMEM((PIECES, 2, 2 * PROWS, half), BF16),
            pltpu.VMEM((PIECES, 2, 2, 2 * PROWS, half), BF16),
            DMA((1 + PIECES,)),
            DMA((PIECES, 2, 4)), DMA((PIECES, 2, 4)),
            DMA((PIECES, 2)), DMA((PIECES, 2)),
            DMA((PIECES, 2, 2)), DMA((PIECES, 2, 2)),
        ],
        compiler_params=pltpu.CompilerParams(
            collective_id=2, has_side_effects=True, vmem_limit_bytes=40 << 20
        ),
        name="project_out",
    )(attended.reshape(PIECES, PROWS, FEAT), w)
    return out.reshape(2 * ROWS, OUTW)


def rope_tables(positions):
    half_dim = HEAD // 2
    lane_ids = jnp.arange(half_dim).astype(F32)
    base_freq = jnp.power(THETA, -2.0 * lane_ids / HEAD)
    wavelen = 2.0 * math.pi / base_freq
    smooth = (8192.0 / wavelen - 1.0) / 3.0
    blended = (1.0 - smooth) * base_freq / 8.0 + smooth * base_freq
    scaled = jnp.where(
        wavelen > 8192.0, base_freq / 8.0, jnp.where(wavelen < 2048.0, base_freq, blended)
    )
    angles = positions.astype(F32)[:, None] * scaled[None, :]
    cos, sin = jnp.cos(angles), jnp.sin(angles)
    return jnp.concatenate([cos, cos], axis=1), jnp.concatenate([-sin, sin], axis=1)


def place(doc_ids, block_order):
    shard = lax.axis_index("blk") * NZ + lax.axis_index("uly")
    per = BLOCK // ROWS
    seq_block = lax.dynamic_index_in_dim(block_order, shard // per, 0, keepdims=False)
    first = seq_block * BLOCK + lax.rem(shard, per) * ROWS
    numbers = jnp.arange(16, dtype=jnp.int32)
    doc_start = jnp.sum((doc_ids[None, :] < numbers[:, None]).astype(jnp.int32), axis=1)
    segment = lax.dynamic_slice_in_dim(doc_ids, first, ROWS)
    q_start = jnp.sum(
        jnp.where(segment[None, :] == numbers[:, None], doc_start[:, None], 0), axis=0
    )
    where_block = jnp.sum(
        jnp.where(block_order[None, :] == numbers[:, None], numbers[None, :], 0), axis=1
    )
    shards = (where_block[:, None] * per + jnp.arange(per, dtype=jnp.int32)[None, :]).reshape(-1)
    q_block = first // ROWS
    head = jnp.stack([q_block - q_start[0] // ROWS + 1, q_block])
    return first, q_start[None, :], jnp.concatenate([head, shards])


def on_device(hidden, norm_gain, query_key_value_weight, w_out, doc_ids, block_order):
    u = lax.axis_index("uly")
    first, q_start, table = place(doc_ids, block_order)
    cos, sin = rope_tables(first + jnp.arange(ROWS, dtype=jnp.int32))
    gain = lax.dynamic_slice_in_dim(norm_gain, u * FEAT, FEAT).astype(F32)[:, None]
    weights = query_key_value_weight.reshape(FEAT, COLS)
    q, kv = project(hidden, weights, gain, cos, sin)
    kv_all = gather_kv(kv)
    attended = attend(table, q, q_start, kv_all)
    return project_out(attended, w_out)


def solution(mesh):
    return jax.shard_map(
        on_device,
        mesh=mesh,
        in_specs=(P(("blk", "uly"), None), P(), P("uly", "tp", None), P("tp", "uly"), P(), P()),
        out_specs=P(("blk", "tp"), "uly"),
        check_vma=False,
    )
```

```python
import math

import jax
import jax.numpy as jnp
import numpy as np
from jax import lax
from jax.experimental import pallas as pl
from jax.experimental.pallas import tpu as pltpu
from jax.sharding import PartitionSpec as P

HEAD = 128
HEADS = 8
BLOCK = 512
THETA = 500000.0
NEG_BIG = -1e30
NZ = 8
NT = 4
ROWS = 128
SUB = ROWS // NT
FEAT = 1024
COLS = (HEADS + 2) * HEAD
MESH = pl.DeviceIdType.MESH
F32 = jnp.float32
BF16 = jnp.bfloat16
FAR_FIRST = (4, 3, 5, 2, 6, 1, 7)
QSCALE = math.log2(math.e) / math.sqrt(HEAD)


def remote(src, dst, send_sem, recv_sem, device):
    return pltpu.make_async_remote_copy(
        src_ref=src,
        dst_ref=dst,
        send_sem=send_sem,
        recv_sem=recv_sem,
        device_id=device,
        device_id_type=MESH,
    )


def greet(devices):
    barrier = pltpu.get_barrier_semaphore()
    for device in devices:
        pl.semaphore_signal(barrier, inc=1, device_id=device, device_id_type=MESH)
    pl.semaphore_wait(barrier, len(devices))


def dot32(a, b):
    return jnp.dot(a, b, preferred_element_type=F32)


KCOL = HEADS * HEAD
PIECE_COLS = (slice(KCOL, KCOL + HEAD), slice(KCOL + HEAD, COLS), slice(0, KCOL // 2), slice(KCOL // 2, KCOL))
QUARTERED = 5
Z_STEPS = (0, -1, 1, -2, 2, -3, 3, -4)


def proj_kernel(
    order, freq, gain, hid, w, q_out, kv_all,
    hloc, wloc, wg, g32, xbuf, own, far, pairs, kv, rope,
    kv_stage, kv_inbox, q_stage, q_inbox,
    lsem, zs, zr, ys, yr, fs, fr, ks, kr, qs, qr,
    gzs, gzr, gxs, gxr, gfs, gfr, gss, gsr,
):
    b = lax.axis_index("blk")
    u = lax.axis_index("uly")
    t = lax.axis_index("tp")
    t_right, t_left, across = lax.rem(t + 1, NT), lax.rem(t + 3, NT), lax.rem(t + 2, NT)
    u_right, u_left = lax.rem(u + 1, NZ), lax.rem(u + NZ - 1, NZ)
    b_right, b_left, b_across = lax.rem(b + 2, 8), lax.rem(b + 6, 8), lax.rem(b + 4, 8)
    sibling = b + 1 - 2 * lax.rem(b, 2)
    load_w = pltpu.make_async_copy(w, wloc, lsem.at[0])
    load_h = pltpu.make_async_copy(hid, hloc, lsem.at[1])
    load_w.start()
    load_h.start()
    greet(
        [{"uly": lax.rem(u + k, NZ)} for k in range(1, NZ)]
        + [{"tp": t_right}, {"tp": t_left}, {"blk": b_right}, {"blk": b_left}, {"blk": sibling}]
    )

    def part(owner):
        return pl.ds(pl.multiple_of(owner * SUB, SUB), SUB)

    def feats(owner):
        return pl.ds(pl.multiple_of(owner * FEAT, FEAT), FEAT)

    over_z = []
    for i, k in enumerate(FAR_FIRST):
        v = lax.rem(u + NZ - k, NZ)
        if i < QUARTERED:
            src, dst = hid.at[part(t), feats(v)], xbuf.at[i, part(t)]
        else:
            src, dst = hid.at[:, feats(v)], xbuf.at[i]
        copy = remote(src, dst, zs.at[i], zr.at[i], {"uly": v})
        copy.start()
        over_z.append(copy)

    g32[...] = gain[...].astype(F32)
    load_w.wait()

    def fold(c, carry):
        r = pl.ds(pl.multiple_of(c * 128, 128), 128)
        column = jnp.broadcast_to(g32[pl.ds(u * NZ + c, 1), :], (128, 128)).T
        for n in range(COLS // 128):
            lanes = slice(n * 128, (n + 1) * 128)
            wg[r, lanes] = (wloc[r, lanes].astype(F32) * column).astype(BF16)
        return carry

    lax.fori_loop(0, FEAT // 128, fold, 0)
    load_h.wait()

    def square(c, acc):
        x = hloc[:, pl.ds(pl.multiple_of(c * 128, 128), 128)].astype(F32)
        return acc + x * x

    def chunk_from(i, source, direction):
        return remote(
            xbuf.at[i, part(source)], xbuf.at[i, part(source)],
            ys.at[i, direction], yr.at[i, direction],
            {"tp": t_right if direction == 0 else t_left},
        )

    def pass_on(i):
        source, target = (t_left, t_right) if i % 2 == 0 else (t_right, t_left)
        return remote(
            xbuf.at[i, part(source)], xbuf.at[i, part(source)], fs.at[i], fr.at[i], {"tp": target}
        )

    def kv_copy(step, direction, piece):
        return remote(
            kv_stage.at[direction, step, piece], kv_inbox.at[direction, step, piece],
            ks.at[direction, step, piece], kr.at[direction, step, piece],
            {"uly": u_right if direction == 0 else u_left},
        )

    def q_copy(step, direction, piece):
        return remote(
            q_stage.at[direction, step, piece], q_inbox.at[direction, step, piece],
            qs.at[direction, step, piece], qr.at[direction, step, piece],
            {"uly": u_right if direction == 0 else u_left},
        )

    def mine(step, direction, cols):
        if step == 0:
            return far[:, cols]
        return pairs[step - 1, direction * ROWS : (direction + 1) * ROWS, cols]

    def send_kv(step, direction, piece):
        value = mine(step, direction, PIECE_COLS[piece])
        if step > 1 or (step == 1 and piece == direction):
            kv_copy(step - 1, direction, piece).wait_recv()
            value = value + kv_inbox[direction, step - 1, piece].astype(F32)
        kv_stage[direction, step, piece] = value.astype(BF16)
        kv_copy(step, direction, piece).start()

    def send_q(step, direction, piece):
        value = mine(step, direction, PIECE_COLS[2 + piece])
        if step > 1 or (step == 1 and piece == direction):
            q_copy(step - 1, direction, piece).wait_recv()
            value = value + q_inbox[direction, step - 1, piece].astype(F32)
        q_stage[direction, step, piece] = value.astype(BF16)
        q_copy(step, direction, piece).start()

    def far_product():
        far[...] = dot32(xbuf[0], wg[...])
        for direction in range(2):
            send_kv(0, direction, direction)
        for direction in range(2):
            send_q(0, direction, direction)

    def pair_product(j):
        x = xbuf[2 * j - 1 : 2 * j + 1].reshape(2 * ROWS, FEAT)
        pairs[j - 1] = dot32(x, wg[...])

    for tick in range(QUARTERED + 2):
        if tick < QUARTERED:
            over_z[tick].wait_recv()
            chunk_from(tick, t, 0).start()
            chunk_from(tick, t, 1).start()
        i = tick - 1
        if 0 <= i < QUARTERED:
            chunk_from(i, t_left, 0).wait_recv()
            chunk_from(i, t_right, 1).wait_recv()
            pass_on(i).start()
        i = tick - 2
        if 0 <= i < QUARTERED:
            remote(
                xbuf.at[i, part(across)], xbuf.at[i, part(across)], fs.at[i], fr.at[i],
                {"tp": t_right},
            ).wait_recv()
            if i == 0:
                far_product()
            elif i % 2 == 0:
                pair_product(i // 2)
            if i == 2:
                for direction in range(2):
                    send_kv(1, direction, 1 - direction)
                    send_kv(1, direction, direction)
                for direction in range(2):
                    send_q(1, direction, 1 - direction)
    for direction in range(2):
        for piece in range(2):
            send_kv(2, direction, piece)
    for direction in range(2):
        send_q(1, direction, direction)
    over_z[QUARTERED].wait_recv()
    over_z[QUARTERED + 1].wait_recv()
    pair_product(3)
    for direction in range(2):
        for piece in range(2):
            send_kv(3, direction, piece)

    total = lax.fori_loop(0, NZ * FEAT // 128, square, jnp.zeros((ROWS, 128), F32))
    scale = lax.rsqrt(jnp.sum(total, axis=1, keepdims=True) / (NZ * FEAT) + 1e-05)
    own[...] = dot32(hloc[:, feats(u)], wg[...])
    shard_id = b * NZ + u
    block = shard_id // (BLOCK // ROWS)
    first = order[block] * BLOCK + lax.rem(shard_id, BLOCK // ROWS) * ROWS
    position = (lax.broadcasted_iota(jnp.int32, (ROWS, HEAD), 0) + first).astype(F32)
    angles = position * freq[...]
    left_half = lax.broadcasted_iota(jnp.int32, (ROWS, HEAD), 1) < HEAD // 2
    sines = jnp.sin(angles)
    rope[0] = jnp.cos(angles)
    rope[1] = jnp.where(left_half, -sines, sines)

    def rotated(x):
        return x * rope[0] + pltpu.roll(x, HEAD // 2, 1) * rope[1]

    for piece in range(2):
        kv_copy(3, 0, piece).wait_recv()
        kv_copy(3, 1, piece).wait_recv()
        x = own[:, PIECE_COLS[piece]]
        x = x + kv_inbox[0, 3, piece].astype(F32)
        x = (x + kv_inbox[1, 3, piece].astype(F32)) * scale
        if piece == 0:
            x = rotated(x)
        kv[:, piece * HEAD : (piece + 1) * HEAD] = x.astype(BF16)

    def z_of(i):
        return lax.rem(u + Z_STEPS[i] + NZ, NZ)

    def shard(owner, i):
        return kv_all.at[owner * NZ + z_of(i)]

    def held(i):
        return kv if i == 0 else shard(b, i)

    def z_copy(i, src, dst):
        to = u_right if Z_STEPS[i] < 0 else u_left
        return remote(src, dst, gzs.at[i], gzr.at[i], {"uly": to})

    def x_send(i, direction):
        return remote(
            held(i), shard(b, i), gxs.at[i, direction], gxr.at[i, direction],
            {"blk": b_right if direction == 0 else b_left},
        )

    def x_wait(i, direction):
        source = b_left if direction == 0 else b_right
        return remote(
            shard(source, i), shard(source, i), gxs.at[i, direction], gxr.at[i, direction],
            {"blk": b_right},
        )

    def x_pass(i):
        source, target = (b_left, b_right) if i % 2 == 0 else (b_right, b_left)
        return remote(shard(source, i), shard(source, i), gfs.at[i], gfr.at[i], {"blk": target})

    def side(i, m):
        owner = (b, b_left, b_right, b_across)[m]
        src = held(i) if m == 0 else shard(owner, i)
        return remote(src, shard(owner, i), gss.at[i, m], gsr.at[i, m], {"blk": sibling})

    def side_wait(i, m):
        owner = lax.rem(sibling + (0, 6, 2, 4)[m], 8)
        return remote(shard(owner, i), shard(owner, i), gss.at[i, m], gsr.at[i, m], {"blk": sibling})

    z_sends = []

    def start_z(step, src_i):
        copy = z_copy(Z_STEPS.index(step), held(src_i), shard(b, src_i))
        copy.start()
        z_sends.append(copy)

    place_own = pltpu.make_async_copy(kv, kv_all.at[b * NZ + u], lsem.at[2])

    def gather_tick(tick):
        i = tick
        if i < NZ:
            step = Z_STEPS[i]
            if i == 0:
                start_z(-1, 0)
                start_z(1, 0)
                place_own.start()
            else:
                z_copy(i, shard(b, i), shard(b, i)).wait_recv()
                if -4 < step < 0:
                    start_z(step - 1, i)
                if 0 < step < 3:
                    start_z(step + 1, i)
            x_send(i, 0).start()
            x_send(i, 1).start()
            side(i, 0).start()
        i = tick - 1
        if 0 <= i < NZ:
            x_wait(i, 0).wait_recv()
            x_wait(i, 1).wait_recv()
            x_pass(i).start()
            side(i, 1).start()
            side(i, 2).start()
        i = tick - 2
        if 0 <= i < NZ:
            remote(
                shard(b_across, i), shard(b_across, i), gfs.at[i], gfr.at[i], {"blk": b_right}
            ).wait_recv()
            side(i, 3).start()

    def finish_q(piece):
        q_copy(3, 0, piece).wait_recv()
        q_copy(3, 1, piece).wait_recv()
        cols = PIECE_COLS[2 + piece]
        x = own[:, cols] + q_inbox[0, 3, piece].astype(F32)
        own[:, cols] = (x + q_inbox[1, 3, piece].astype(F32)) * (scale * QSCALE)
        for h in range(piece * HEADS // 2, (piece + 1) * HEADS // 2):
            x = rotated(own[:, h * HEAD : (h + 1) * HEAD])
            q_out[h * ROWS : (h + 1) * ROWS, :] = x.astype(BF16)

    gather_tick(0)
    for direction in range(2):
        send_q(2, direction, direction)
    gather_tick(1)
    for direction in range(2):
        send_q(2, direction, 1 - direction)
    gather_tick(2)
    gather_tick(3)
    for direction in range(2):
        send_q(3, direction, direction)
    gather_tick(4)
    for direction in range(2):
        send_q(3, direction, 1 - direction)
    gather_tick(5)
    gather_tick(6)
    finish_q(0)
    gather_tick(7)
    finish_q(1)
    gather_tick(8)
    gather_tick(9)
    place_own.wait()
    for i in range(NZ):
        for m in range(4):
            side_wait(i, m).wait_recv()

    for copy in over_z:
        copy.wait_send()
    for i in range(QUARTERED):
        chunk_from(i, t, 0).wait_send()
        chunk_from(i, t, 1).wait_send()
        pass_on(i).wait_send()
    for direction in range(2):
        for step in range(4):
            for piece in range(2):
                if step > 0 or piece == direction:
                    kv_copy(step, direction, piece).wait_send()
                    q_copy(step, direction, piece).wait_send()
    for copy in z_sends:
        copy.wait_send()
    for i in range(NZ):
        x_send(i, 0).wait_send()
        x_send(i, 1).wait_send()
        x_pass(i).wait_send()
        for m in range(4):
            side(i, m).wait_send()


ANY = pl.BlockSpec(memory_space=pl.ANY)
VM = pl.BlockSpec(memory_space=pltpu.VMEM)
DMA = pltpu.SemaphoreType.DMA


HBM = pl.BlockSpec(memory_space=pltpu.HBM)
SM = pl.BlockSpec(memory_space=pltpu.SMEM)


def project(order, freq, gain, hidden, weights):
    n = NZ - 1
    return pl.pallas_call(
        proj_kernel,
        out_shape=(
            jax.ShapeDtypeStruct((HEADS * ROWS, HEAD), BF16),
            jax.ShapeDtypeStruct((8 * NZ, ROWS, 2 * HEAD), BF16),
        ),
        in_specs=[SM, VM, VM, HBM, HBM],
        out_specs=(VM, VM),
        scratch_shapes=[
            pltpu.VMEM((ROWS, NZ * FEAT), BF16),
            pltpu.VMEM((FEAT, COLS), BF16),
            pltpu.VMEM((FEAT, COLS), BF16),
            pltpu.VMEM((NZ * FEAT // 128, 128), F32),
            pltpu.VMEM((n, ROWS, FEAT), BF16),
            pltpu.VMEM((ROWS, COLS), F32),
            pltpu.VMEM((ROWS, COLS), F32),
            pltpu.VMEM((3, 2 * ROWS, COLS), F32),
            pltpu.VMEM((ROWS, 2 * HEAD), BF16),
            pltpu.VMEM((2, ROWS, HEAD), F32),
            pltpu.VMEM((2, 4, 2, ROWS, HEAD), BF16),
            pltpu.VMEM((2, 4, 2, ROWS, HEAD), BF16),
            pltpu.VMEM((2, 4, 2, ROWS, KCOL // 2), BF16),
            pltpu.VMEM((2, 4, 2, ROWS, KCOL // 2), BF16),
            DMA((3,)),
            DMA((n,)), DMA((n,)),
            DMA((n, 2)), DMA((n, 2)),
            DMA((n,)), DMA((n,)),
            DMA((2, 4, 2)), DMA((2, 4, 2)),
            DMA((2, 4, 2)), DMA((2, 4, 2)),
            DMA((NZ,)), DMA((NZ,)),
            DMA((NZ, 2)), DMA((NZ, 2)),
            DMA((NZ,)), DMA((NZ,)),
            DMA((NZ, 4)), DMA((NZ, 4)),
        ],
        compiler_params=pltpu.CompilerParams(
            collective_id=0, has_side_effects=True, vmem_limit_bytes=62 << 20
        ),
        name="project",
    )(order, freq, gain, hidden, weights)


def attend_kernel(order, docs, q, kv, out, inverse, m_ref, l_ref, acc):
    per = BLOCK // ROWS
    shard = lax.axis_index("blk") * NZ + lax.axis_index("uly")
    q_block = order[shard // per] * per + lax.rem(shard, per)
    for r in range(16):
        inverse[order[r]] = r
    segment = docs[pl.ds(q_block, 1), :]
    starts = jnp.zeros((1, ROWS), jnp.int32)
    for n in range(1, 16):
        before = jnp.sum((docs[...] < n).astype(jnp.int32))
        starts = jnp.where(segment == n, before, starts)
    count = q_block - jnp.min(starts) // ROWS + 1
    wide = HEADS * ROWS
    m_ref[...] = jnp.full((1, wide), NEG_BIG, F32)
    l_ref[...] = jnp.zeros((1, wide), F32)
    acc[...] = jnp.zeros((HEAD, wide), F32)
    lane = lax.broadcasted_iota(jnp.int32, (128, ROWS), 1)
    row = lax.broadcasted_iota(jnp.int32, (128, ROWS), 0)
    causal = row <= lane
    starts = jnp.broadcast_to(starts, (128, ROWS))

    def step(i, carry):
        k_block = q_block - i
        at = inverse[k_block // per] * per + lax.rem(k_block, per)
        k = kv[at, :, :HEAD]
        v = kv[at, :, HEAD:]
        scores = lax.dot_general(
            k, q[...], (((1,), (1,)), ((), ())), preferred_element_type=F32
        )
        allowed = (row + k_block * 128 >= starts) & (causal | (i > 0))
        bias = jnp.where(allowed, 0.0, NEG_BIG)
        scores = scores + jnp.concatenate([bias] * HEADS, axis=1)
        m_old = m_ref[...]
        m_new = jnp.maximum(m_old, jnp.max(scores, axis=0, keepdims=True))
        weights = jnp.exp2(scores - m_new)
        factor = jnp.exp2(m_old - m_new)
        m_ref[...] = m_new
        l_ref[...] = l_ref[...] * factor + jnp.sum(weights, axis=0, keepdims=True)
        mixed = lax.dot_general(
            v, weights.astype(BF16), (((0,), (0,)), ((), ())), preferred_element_type=F32
        )
        acc[...] = acc[...] * factor + mixed
        return carry

    lax.fori_loop(0, count, step, 0)
    result = acc[...] / l_ref[...]
    for h in range(HEADS):
        part = result[:, h * ROWS : (h + 1) * ROWS]
        out[:, h * HEAD : (h + 1) * HEAD] = part.T.astype(BF16)


def attend(order, docs, q, kv):
    wide = HEADS * ROWS
    return pl.pallas_call(
        attend_kernel,
        out_shape=jax.ShapeDtypeStruct((ROWS, HEADS * HEAD), BF16),
        in_specs=[SM, VM, VM, VM],
        out_specs=VM,
        scratch_shapes=[
            pltpu.SMEM((16,), jnp.int32),
            pltpu.VMEM((1, wide), F32),
            pltpu.VMEM((1, wide), F32),
            pltpu.VMEM((HEAD, wide), F32),
        ],
        compiler_params=pltpu.CompilerParams(vmem_limit_bytes=60 << 20),
        name="attend",
    )(order, docs, q, kv)


PIECES = 2
PROWS = ROWS // PIECES
OUTW = 1024


def out_kernel(att, w, out, wloc, abuf, far_stage, near_stage, far_box, near_box,
               lsem, zs, zr, fs, fr, ns, nr):
    u = lax.axis_index("uly")
    t = lax.axis_index("tp")
    t_right, t_left = lax.rem(t + 1, NT), lax.rem(t + NT - 1, NT)
    u_right, u_left = lax.rem(u + 1, NZ), lax.rem(u + NZ - 1, NZ)
    load_w = pltpu.make_async_copy(w, wloc, lsem.at[0])
    load_w.start()
    own_copies = []
    for p in range(PIECES):
        copy = pltpu.make_async_copy(att.at[p], abuf.at[u, p], lsem.at[1 + p])
        copy.start()
        own_copies.append(copy)
    greet([{"uly": u_right}, {"uly": u_left}, {"tp": t_right}, {"tp": t_left}])

    def z_hops(p, direction):
        return 4 if (p + direction) % 2 == 0 else 3

    def chunk(direction, h):
        return lax.rem(u + NZ + (-h if direction == 0 else h), NZ)

    def z_copy(p, direction, h, source):
        src = att.at[p] if h == 0 else abuf.at[source, p]
        return remote(
            src, abuf.at[source, p], zs.at[p, direction, h], zr.at[p, direction, h],
            {"uly": u_right if direction == 0 else u_left},
        )

    def z_send(p, direction, h):
        return z_copy(p, direction, h, chunk(direction, h))

    def z_wait(p, direction, h):
        source = chunk(direction, h + 1)
        return remote(
            abuf.at[source, p], abuf.at[source, p], zs.at[p, direction, h],
            zr.at[p, direction, h], {"uly": u_right},
        )

    def z_step(p, h):
        for direction in range(2):
            hops = z_hops(p, direction)
            if h > 0 and h <= hops:
                z_wait(p, direction, h - 1).wait_recv()
            if h < hops:
                z_send(p, direction, h).start()

    def product(p, rel):
        d = lax.rem(t + rel, NT)
        x = abuf[pl.ds(2 * d, 2), p].reshape(2 * PROWS, FEAT)
        return dot32(x, wloc[...])

    def half(side):
        return slice(side * (OUTW // 2), (side + 1) * (OUTW // 2))

    def far_send(p, side):
        return remote(
            far_stage.at[p, side], far_box.at[p, side], fs.at[p, side], fr.at[p, side],
            {"tp": t_right if side == 0 else t_left},
        )

    def near_send(p, direction, side):
        return remote(
            near_stage.at[p, direction, side], near_box.at[p, direction, side],
            ns.at[p, direction, side], nr.at[p, direction, side],
            {"tp": t_right if direction == 0 else t_left},
        )

    for p in range(PIECES):
        z_step(p, 0)
    load_w.wait()
    for copy in own_copies:
        copy.wait()
    for h in range(1, 5):
        z_step(0, h)
    for p in range(PIECES):
        more = p + 1 < PIECES
        value = product(p, 2)
        for side in range(2):
            far_stage[p, side] = value[:, half(side)].astype(BF16)
            far_send(p, side).start()
        if more:
            z_step(p + 1, 1)
        right = product(p, 1)
        near_stage[p, 0, 1] = right[:, half(1)].astype(BF16)
        near_send(p, 0, 1).start()
        left = product(p, 3)
        near_stage[p, 1, 0] = left[:, half(0)].astype(BF16)
        near_send(p, 1, 0).start()
        if more:
            z_step(p + 1, 2)
        far_send(p, 0).wait_recv()
        near_stage[p, 0, 0] = (right[:, half(0)] + far_box[p, 0].astype(F32)).astype(BF16)
        near_send(p, 0, 0).start()
        far_send(p, 1).wait_recv()
        near_stage[p, 1, 1] = (left[:, half(1)] + far_box[p, 1].astype(F32)).astype(BF16)
        near_send(p, 1, 1).start()
        if more:
            z_step(p + 1, 3)
        mine = product(p, 0)
        if more:
            z_step(p + 1, 4)
        for side in range(2):
            near_send(p, 0, side).wait_recv()
            near_send(p, 1, side).wait_recv()
            summed = mine[:, half(side)] + near_box[p, 0, side].astype(F32)
            summed = summed + near_box[p, 1, side].astype(F32)
            out[:, p, :, half(side)] = summed.reshape(2, PROWS, OUTW // 2).astype(BF16)
    for p in range(PIECES):
        for direction in range(2):
            for h in range(z_hops(p, direction)):
                z_send(p, direction, h).wait_send()
            far_send(p, direction).wait_send()
            for side in range(2):
                near_send(p, direction, side).wait_send()


def project_out(attended, w):
    half = OUTW // 2
    out = pl.pallas_call(
        out_kernel,
        out_shape=jax.ShapeDtypeStruct((2, PIECES, PROWS, OUTW), BF16),
        in_specs=[ANY, HBM],
        out_specs=VM,
        scratch_shapes=[
            pltpu.VMEM((FEAT, OUTW), BF16),
            pltpu.VMEM((NZ, PIECES, PROWS, FEAT), BF16),
            pltpu.VMEM((PIECES, 2, 2 * PROWS, half), BF16),
            pltpu.VMEM((PIECES, 2, 2, 2 * PROWS, half), BF16),
            pltpu.VMEM((PIECES, 2, 2 * PROWS, half), BF16),
            pltpu.VMEM((PIECES, 2, 2, 2 * PROWS, half), BF16),
            DMA((1 + PIECES,)),
            DMA((PIECES, 2, 4)), DMA((PIECES, 2, 4)),
            DMA((PIECES, 2)), DMA((PIECES, 2)),
            DMA((PIECES, 2, 2)), DMA((PIECES, 2, 2)),
        ],
        compiler_params=pltpu.CompilerParams(
            collective_id=2, has_side_effects=True, vmem_limit_bytes=62 << 20
        ),
        name="project_out",
    )(attended.reshape(PIECES, PROWS, FEAT), w)
    return out.reshape(2 * ROWS, OUTW)


def rope_frequencies():
    base = THETA ** (-2.0 * np.arange(HEAD // 2, dtype=np.float64) / HEAD)
    wavelen = 2.0 * np.pi / base
    smooth = (8192.0 / wavelen - 1.0) / 3.0
    blended = (1.0 - smooth) * base / 8.0 + smooth * base
    scaled = np.where(wavelen > 8192.0, base / 8.0, np.where(wavelen < 2048.0, base, blended))
    return jnp.asarray(np.tile(scaled, 2)[None, :], F32)


def on_device(hidden, norm_gain, query_key_value_weight, w_out, doc_ids, block_order):
    weights = query_key_value_weight.reshape(FEAT, COLS)
    gain = norm_gain.reshape(NZ * FEAT // 128, 128)
    docs = doc_ids.reshape(NZ * FEAT // 128, 128)
    q, kv_all = project(block_order, rope_frequencies(), gain, hidden, weights)
    attended = attend(block_order, docs, q, kv_all)
    return project_out(attended, w_out)


def solution(mesh):
    return jax.shard_map(
        on_device,
        mesh=mesh,
        in_specs=(P(("blk", "uly"), None), P(), P("uly", "tp", None), P("tp", "uly"), P(), P()),
        out_specs=P(("blk", "tp"), "uly"),
        check_vma=False,
    )
```

```python
import math

import jax
import jax.numpy as jnp
import numpy as np
from jax import lax
from jax.experimental import pallas as pl
from jax.experimental.pallas import tpu as pltpu
from jax.sharding import PartitionSpec as P

HEAD = 128
HEADS = 8
BLOCK = 512
THETA = 500000.0
NEG_BIG = -1e30
NZ = 8
NT = 4
ROWS = 128
SUB = ROWS // NT
FEAT = 1024
COLS = (HEADS + 2) * HEAD
MESH = pl.DeviceIdType.MESH
F32 = jnp.float32
BF16 = jnp.bfloat16
FAR_FIRST = (4, 3, 5, 2, 6, 1, 7)
QSCALE = math.log2(math.e) / math.sqrt(HEAD)


def remote(src, dst, send_sem, recv_sem, device):
    return pltpu.make_async_remote_copy(
        src_ref=src,
        dst_ref=dst,
        send_sem=send_sem,
        recv_sem=recv_sem,
        device_id=device,
        device_id_type=MESH,
    )


def greet(devices):
    barrier = pltpu.get_barrier_semaphore()
    for device in devices:
        pl.semaphore_signal(barrier, inc=1, device_id=device, device_id_type=MESH)
    pl.semaphore_wait(barrier, len(devices))


def dot32(a, b):
    return jnp.dot(a, b, preferred_element_type=F32)


KCOL = HEADS * HEAD
PIECE_COLS = (slice(KCOL, KCOL + HEAD), slice(KCOL + HEAD, COLS), slice(0, KCOL // 2), slice(KCOL // 2, KCOL))
QUARTERED = 5
Z_STEPS = (0, -1, 1, -2, 2, -3, 3, -4)


def proj_kernel(
    order, freq, gain, hid, w, q_out, kv_all,
    hloc, wloc, wg, g32, xbuf, own, far, pairs, kv, rope, row_scale,
    kv_stage, kv_inbox, q_stage, q_inbox,
    lsem, zs, zr, ys, yr, fs, fr, ks, kr, qs, qr,
    gzs, gzr, gxs, gxr, gfs, gfr, gss, gsr,
):
    b = lax.axis_index("blk")
    u = lax.axis_index("uly")
    t = lax.axis_index("tp")
    t_right, t_left, across = lax.rem(t + 1, NT), lax.rem(t + 3, NT), lax.rem(t + 2, NT)
    u_right, u_left = lax.rem(u + 1, NZ), lax.rem(u + NZ - 1, NZ)
    b_right, b_left, b_across = lax.rem(b + 2, 8), lax.rem(b + 6, 8), lax.rem(b + 4, 8)
    sibling = b + 1 - 2 * lax.rem(b, 2)
    load_w = pltpu.make_async_copy(w, wloc, lsem.at[0])
    load_h = pltpu.make_async_copy(hid, hloc, lsem.at[1])
    load_w.start()
    load_h.start()
    greet(
        [{"uly": lax.rem(u + k, NZ)} for k in range(1, NZ)]
        + [{"tp": t_right}, {"tp": t_left}, {"blk": b_right}, {"blk": b_left}, {"blk": sibling}]
    )

    def part(owner):
        return pl.ds(pl.multiple_of(owner * SUB, SUB), SUB)

    def feats(owner):
        return pl.ds(pl.multiple_of(owner * FEAT, FEAT), FEAT)

    over_z = []
    for i, k in enumerate(FAR_FIRST):
        v = lax.rem(u + NZ - k, NZ)
        if i < QUARTERED:
            src, dst = hid.at[part(t), feats(v)], xbuf.at[i, part(t)]
        else:
            src, dst = hid.at[:, feats(v)], xbuf.at[i]
        copy = remote(src, dst, zs.at[i], zr.at[i], {"uly": v})
        copy.start()
        over_z.append(copy)

    g32[...] = gain[...].astype(F32)
    load_w.wait()

    def fold(c, carry):
        r = pl.ds(pl.multiple_of(c * 128, 128), 128)
        column = jnp.broadcast_to(g32[pl.ds(u * NZ + c, 1), :], (128, 128)).T
        for n in range(COLS // 128):
            lanes = slice(n * 128, (n + 1) * 128)
            wg[r, lanes] = (wloc[r, lanes].astype(F32) * column).astype(BF16)
        return carry

    lax.fori_loop(0, FEAT // 128, fold, 0)
    load_h.wait()

    def square(c, acc):
        x = hloc[:, pl.ds(pl.multiple_of(c * 128, 128), 128)].astype(F32)
        return acc + x * x

    total = lax.fori_loop(0, NZ * FEAT // 128, square, jnp.zeros((ROWS, 128), F32))
    mean = jnp.sum(total, axis=1, keepdims=True) / (NZ * FEAT)
    row_scale[...] = jnp.broadcast_to(lax.rsqrt(mean + 1e-05), (ROWS, HEAD))
    shard_id = b * NZ + u
    block = shard_id // (BLOCK // ROWS)
    first = order[block] * BLOCK + lax.rem(shard_id, BLOCK // ROWS) * ROWS
    position = (lax.broadcasted_iota(jnp.int32, (ROWS, HEAD), 0) + first).astype(F32)
    angles = position * freq[...]
    left_half = lax.broadcasted_iota(jnp.int32, (ROWS, HEAD), 1) < HEAD // 2
    sines = jnp.sin(angles)
    rope[0] = jnp.cos(angles)
    rope[1] = jnp.where(left_half, -sines, sines)

    def chunk_from(i, source, direction):
        return remote(
            xbuf.at[i, part(source)], xbuf.at[i, part(source)],
            ys.at[i, direction], yr.at[i, direction],
            {"tp": t_right if direction == 0 else t_left},
        )

    def pass_on(i):
        source, target = (t_left, t_right) if i % 2 == 0 else (t_right, t_left)
        return remote(
            xbuf.at[i, part(source)], xbuf.at[i, part(source)], fs.at[i], fr.at[i], {"tp": target}
        )

    def kv_copy(step, direction, piece):
        return remote(
            kv_stage.at[direction, step, piece], kv_inbox.at[direction, step, piece],
            ks.at[direction, step, piece], kr.at[direction, step, piece],
            {"uly": u_right if direction == 0 else u_left},
        )

    def q_copy(step, direction, piece):
        return remote(
            q_stage.at[direction, step, piece], q_inbox.at[direction, step, piece],
            qs.at[direction, step, piece], qr.at[direction, step, piece],
            {"uly": u_right if direction == 0 else u_left},
        )

    def mine(step, direction, cols):
        if step == 0:
            return far[:, cols]
        return pairs[step - 1, direction * ROWS : (direction + 1) * ROWS, cols]

    def send_kv(step, direction, piece):
        value = mine(step, direction, PIECE_COLS[piece])
        if step > 1 or (step == 1 and piece == direction):
            kv_copy(step - 1, direction, piece).wait_recv()
            value = value + kv_inbox[direction, step - 1, piece].astype(F32)
        kv_stage[direction, step, piece] = value.astype(BF16)
        kv_copy(step, direction, piece).start()

    def send_q(step, direction, piece):
        value = mine(step, direction, PIECE_COLS[2 + piece])
        if step > 1 or (step == 1 and piece == direction):
            q_copy(step - 1, direction, piece).wait_recv()
            value = value + q_inbox[direction, step - 1, piece].astype(F32)
        q_stage[direction, step, piece] = value.astype(BF16)
        q_copy(step, direction, piece).start()

    def far_product():
        far[...] = dot32(xbuf[0], wg[...])
        for direction in range(2):
            send_kv(0, direction, direction)

    def pair_product(j):
        x = xbuf[2 * j - 1 : 2 * j + 1].reshape(2 * ROWS, FEAT)
        pairs[j - 1] = dot32(x, wg[...])

    for tick in range(QUARTERED + 2):
        if tick < QUARTERED:
            over_z[tick].wait_recv()
            chunk_from(tick, t, 0).start()
            chunk_from(tick, t, 1).start()
        if tick == 0:
            own[...] = dot32(hloc[:, feats(u)], wg[...])
        i = tick - 1
        if 0 <= i < QUARTERED:
            chunk_from(i, t_left, 0).wait_recv()
            chunk_from(i, t_right, 1).wait_recv()
            pass_on(i).start()
        i = tick - 2
        if 0 <= i < QUARTERED:
            remote(
                xbuf.at[i, part(across)], xbuf.at[i, part(across)], fs.at[i], fr.at[i],
                {"tp": t_right},
            ).wait_recv()
            if i == 0:
                far_product()
            elif i % 2 == 0:
                pair_product(i // 2)
            if i == 2:
                for direction in range(2):
                    send_kv(1, direction, 1 - direction)
                    send_kv(1, direction, direction)
                for direction in range(2):
                    send_q(0, direction, direction)
                for direction in range(2):
                    send_q(1, direction, 1 - direction)
    for direction in range(2):
        for piece in range(2):
            send_kv(2, direction, piece)
    over_z[QUARTERED].wait_recv()
    over_z[QUARTERED + 1].wait_recv()
    pair_product(3)
    for direction in range(2):
        for piece in range(2):
            send_kv(3, direction, piece)
    for direction in range(2):
        send_q(1, direction, direction)

    def rotated(x):
        return x * rope[0] + pltpu.roll(x, HEAD // 2, 1) * rope[1]

    for piece in range(2):
        kv_copy(3, 0, piece).wait_recv()
        kv_copy(3, 1, piece).wait_recv()
        x = own[:, PIECE_COLS[piece]]
        x = x + kv_inbox[0, 3, piece].astype(F32)
        x = (x + kv_inbox[1, 3, piece].astype(F32)) * row_scale[...]
        if piece == 0:
            x = rotated(x)
        kv[:, piece * HEAD : (piece + 1) * HEAD] = x.astype(BF16)

    def z_of(i):
        return lax.rem(u + Z_STEPS[i] + NZ, NZ)

    def shard(owner, i):
        return kv_all.at[owner * NZ + z_of(i)]

    def held(i):
        return kv if i == 0 else shard(b, i)

    def z_copy(i, src, dst):
        to = u_right if Z_STEPS[i] < 0 else u_left
        return remote(src, dst, gzs.at[i], gzr.at[i], {"uly": to})

    def x_send(i, direction):
        return remote(
            held(i), shard(b, i), gxs.at[i, direction], gxr.at[i, direction],
            {"blk": b_right if direction == 0 else b_left},
        )

    def x_wait(i, direction):
        source = b_left if direction == 0 else b_right
        return remote(
            shard(source, i), shard(source, i), gxs.at[i, direction], gxr.at[i, direction],
            {"blk": b_right},
        )

    def x_pass(i):
        source, target = (b_left, b_right) if i % 2 == 0 else (b_right, b_left)
        return remote(shard(source, i), shard(source, i), gfs.at[i], gfr.at[i], {"blk": target})

    def side(i, m):
        owner = (b, b_left, b_right, b_across)[m]
        src = held(i) if m == 0 else shard(owner, i)
        return remote(src, shard(owner, i), gss.at[i, m], gsr.at[i, m], {"blk": sibling})

    def side_wait(i, m):
        owner = lax.rem(sibling + (0, 6, 2, 4)[m], 8)
        return remote(shard(owner, i), shard(owner, i), gss.at[i, m], gsr.at[i, m], {"blk": sibling})

    z_sends = []

    def start_z(step, src_i):
        copy = z_copy(Z_STEPS.index(step), held(src_i), shard(b, src_i))
        copy.start()
        z_sends.append(copy)

    place_own = pltpu.make_async_copy(kv, kv_all.at[b * NZ + u], lsem.at[2])

    def gather_tick(tick):
        i = tick
        if i < NZ:
            step = Z_STEPS[i]
            if i == 0:
                start_z(-1, 0)
                start_z(1, 0)
                place_own.start()
            else:
                z_copy(i, shard(b, i), shard(b, i)).wait_recv()
                if -4 < step < 0:
                    start_z(step - 1, i)
                if 0 < step < 3:
                    start_z(step + 1, i)
            x_send(i, 0).start()
            x_send(i, 1).start()
            side(i, 0).start()
        i = tick - 1
        if 0 <= i < NZ:
            x_wait(i, 0).wait_recv()
            x_wait(i, 1).wait_recv()
            x_pass(i).start()
            side(i, 1).start()
            side(i, 2).start()
        i = tick - 2
        if 0 <= i < NZ:
            remote(
                shard(b_across, i), shard(b_across, i), gfs.at[i], gfr.at[i], {"blk": b_right}
            ).wait_recv()
            side(i, 3).start()

    def finish_q(piece):
        q_copy(3, 0, piece).wait_recv()
        q_copy(3, 1, piece).wait_recv()
        cols = PIECE_COLS[2 + piece]
        x = own[:, cols] + q_inbox[0, 3, piece].astype(F32)
        own[:, cols] = (x + q_inbox[1, 3, piece].astype(F32)) * (row_scale[:, :1] * QSCALE)
        for h in range(piece * HEADS // 2, (piece + 1) * HEADS // 2):
            x = rotated(own[:, h * HEAD : (h + 1) * HEAD])
            q_out[h * ROWS : (h + 1) * ROWS, :] = x.astype(BF16)

    gather_tick(0)
    for direction in range(2):
        send_q(2, direction, 1 - direction)
    gather_tick(1)
    for direction in range(2):
        send_q(2, direction, direction)
    gather_tick(2)
    gather_tick(3)
    for direction in range(2):
        send_q(3, direction, 1 - direction)
    gather_tick(4)
    for direction in range(2):
        send_q(3, direction, direction)
    gather_tick(5)
    gather_tick(6)
    finish_q(0)
    gather_tick(7)
    finish_q(1)
    gather_tick(8)
    gather_tick(9)
    place_own.wait()
    for i in range(NZ):
        for m in range(4):
            side_wait(i, m).wait_recv()

    for copy in over_z:
        copy.wait_send()
    for i in range(QUARTERED):
        chunk_from(i, t, 0).wait_send()
        chunk_from(i, t, 1).wait_send()
        pass_on(i).wait_send()
    for direction in range(2):
        for step in range(4):
            for piece in range(2):
                if step > 0 or piece == direction:
                    kv_copy(step, direction, piece).wait_send()
                    q_copy(step, direction, piece).wait_send()
    for copy in z_sends:
        copy.wait_send()
    for i in range(NZ):
        x_send(i, 0).wait_send()
        x_send(i, 1).wait_send()
        x_pass(i).wait_send()
        for m in range(4):
            side(i, m).wait_send()


ANY = pl.BlockSpec(memory_space=pl.ANY)
VM = pl.BlockSpec(memory_space=pltpu.VMEM)
DMA = pltpu.SemaphoreType.DMA


HBM = pl.BlockSpec(memory_space=pltpu.HBM)
SM = pl.BlockSpec(memory_space=pltpu.SMEM)


def project(order, freq, gain, hidden, weights):
    n = NZ - 1
    return pl.pallas_call(
        proj_kernel,
        out_shape=(
            jax.ShapeDtypeStruct((HEADS * ROWS, HEAD), BF16),
            jax.ShapeDtypeStruct((8 * NZ, ROWS, 2 * HEAD), BF16),
        ),
        in_specs=[SM, VM, VM, HBM, HBM],
        out_specs=(VM, VM),
        scratch_shapes=[
            pltpu.VMEM((ROWS, NZ * FEAT), BF16),
            pltpu.VMEM((FEAT, COLS), BF16),
            pltpu.VMEM((FEAT, COLS), BF16),
            pltpu.VMEM((NZ * FEAT // 128, 128), F32),
            pltpu.VMEM((n, ROWS, FEAT), BF16),
            pltpu.VMEM((ROWS, COLS), F32),
            pltpu.VMEM((ROWS, COLS), F32),
            pltpu.VMEM((3, 2 * ROWS, COLS), F32),
            pltpu.VMEM((ROWS, 2 * HEAD), BF16),
            pltpu.VMEM((2, ROWS, HEAD), F32),
            pltpu.VMEM((ROWS, HEAD), F32),
            pltpu.VMEM((2, 4, 2, ROWS, HEAD), BF16),
            pltpu.VMEM((2, 4, 2, ROWS, HEAD), BF16),
            pltpu.VMEM((2, 4, 2, ROWS, KCOL // 2), BF16),
            pltpu.VMEM((2, 4, 2, ROWS, KCOL // 2), BF16),
            DMA((3,)),
            DMA((n,)), DMA((n,)),
            DMA((n, 2)), DMA((n, 2)),
            DMA((n,)), DMA((n,)),
            DMA((2, 4, 2)), DMA((2, 4, 2)),
            DMA((2, 4, 2)), DMA((2, 4, 2)),
            DMA((NZ,)), DMA((NZ,)),
            DMA((NZ, 2)), DMA((NZ, 2)),
            DMA((NZ,)), DMA((NZ,)),
            DMA((NZ, 4)), DMA((NZ, 4)),
        ],
        compiler_params=pltpu.CompilerParams(
            collective_id=0, has_side_effects=True, vmem_limit_bytes=62 << 20
        ),
        name="project",
    )(order, freq, gain, hidden, weights)


def attend_kernel(order, docs, q, kv, out, inverse, m_ref, l_ref, acc):
    per = BLOCK // ROWS
    shard = lax.axis_index("blk") * NZ + lax.axis_index("uly")
    q_block = order[shard // per] * per + lax.rem(shard, per)
    for r in range(16):
        inverse[order[r]] = r
    segment = docs[pl.ds(q_block, 1), :]
    starts = jnp.zeros((1, ROWS), jnp.int32)
    for n in range(1, 16):
        before = jnp.sum((docs[...] < n).astype(jnp.int32))
        starts = jnp.where(segment == n, before, starts)
    count = q_block - jnp.min(starts) // ROWS + 1
    wide = HEADS * ROWS
    m_ref[...] = jnp.full((1, wide), NEG_BIG, F32)
    l_ref[...] = jnp.zeros((1, wide), F32)
    acc[...] = jnp.zeros((HEAD, wide), F32)
    lane = lax.broadcasted_iota(jnp.int32, (128, ROWS), 1)
    row = lax.broadcasted_iota(jnp.int32, (128, ROWS), 0)
    causal = row <= lane
    starts = jnp.broadcast_to(starts, (128, ROWS))

    def step(i, carry):
        k_block = q_block - i
        at = inverse[k_block // per] * per + lax.rem(k_block, per)
        k = kv[at, :, :HEAD]
        v = kv[at, :, HEAD:]
        scores = lax.dot_general(
            k, q[...], (((1,), (1,)), ((), ())), preferred_element_type=F32
        )
        allowed = (row + k_block * 128 >= starts) & (causal | (i > 0))
        bias = jnp.where(allowed, 0.0, NEG_BIG)
        scores = scores + jnp.concatenate([bias] * HEADS, axis=1)
        m_old = m_ref[...]
        m_new = jnp.maximum(m_old, jnp.max(scores, axis=0, keepdims=True))
        weights = jnp.exp2(scores - m_new)
        factor = jnp.exp2(m_old - m_new)
        m_ref[...] = m_new
        l_ref[...] = l_ref[...] * factor + jnp.sum(weights, axis=0, keepdims=True)
        mixed = lax.dot_general(
            v, weights.astype(BF16), (((0,), (0,)), ((), ())), preferred_element_type=F32
        )
        acc[...] = acc[...] * factor + mixed
        return carry

    lax.fori_loop(0, count, step, 0)
    result = acc[...] / l_ref[...]
    for h in range(HEADS):
        part = result[:, h * ROWS : (h + 1) * ROWS]
        out[:, h * HEAD : (h + 1) * HEAD] = part.T.astype(BF16)


def attend(order, docs, q, kv):
    wide = HEADS * ROWS
    return pl.pallas_call(
        attend_kernel,
        out_shape=jax.ShapeDtypeStruct((ROWS, HEADS * HEAD), BF16),
        in_specs=[SM, VM, VM, VM],
        out_specs=VM,
        scratch_shapes=[
            pltpu.SMEM((16,), jnp.int32),
            pltpu.VMEM((1, wide), F32),
            pltpu.VMEM((1, wide), F32),
            pltpu.VMEM((HEAD, wide), F32),
        ],
        compiler_params=pltpu.CompilerParams(vmem_limit_bytes=60 << 20),
        name="attend",
    )(order, docs, q, kv)


PIECES = 2
PROWS = ROWS // PIECES
OUTW = 1024


def out_kernel(att, w, out, wloc, abuf, far_stage, near_stage, far_box, near_box,
               lsem, zs, zr, fs, fr, ns, nr):
    u = lax.axis_index("uly")
    t = lax.axis_index("tp")
    t_right, t_left = lax.rem(t + 1, NT), lax.rem(t + NT - 1, NT)
    u_right, u_left = lax.rem(u + 1, NZ), lax.rem(u + NZ - 1, NZ)
    load_w = pltpu.make_async_copy(w, wloc, lsem.at[0])
    load_w.start()
    own_copies = []
    for p in range(PIECES):
        copy = pltpu.make_async_copy(att.at[p], abuf.at[u, p], lsem.at[1 + p])
        copy.start()
        own_copies.append(copy)
    greet([{"uly": u_right}, {"uly": u_left}, {"tp": t_right}, {"tp": t_left}])

    def z_hops(p, direction):
        return 4 if (p + direction) % 2 == 0 else 3

    def chunk(direction, h):
        return lax.rem(u + NZ + (-h if direction == 0 else h), NZ)

    def z_copy(p, direction, h, source):
        src = att.at[p] if h == 0 else abuf.at[source, p]
        return remote(
            src, abuf.at[source, p], zs.at[p, direction, h], zr.at[p, direction, h],
            {"uly": u_right if direction == 0 else u_left},
        )

    def z_send(p, direction, h):
        return z_copy(p, direction, h, chunk(direction, h))

    def z_wait(p, direction, h):
        source = chunk(direction, h + 1)
        return remote(
            abuf.at[source, p], abuf.at[source, p], zs.at[p, direction, h],
            zr.at[p, direction, h], {"uly": u_right},
        )

    def z_step(p, h):
        for direction in range(2):
            hops = z_hops(p, direction)
            if h > 0 and h <= hops:
                z_wait(p, direction, h - 1).wait_recv()
            if h < hops:
                z_send(p, direction, h).start()

    def product(p, rel):
        d = lax.rem(t + rel, NT)
        x = abuf[pl.ds(2 * d, 2), p].reshape(2 * PROWS, FEAT)
        return dot32(x, wloc[...])

    def half(side):
        return slice(side * (OUTW // 2), (side + 1) * (OUTW // 2))

    def far_send(p, side):
        return remote(
            far_stage.at[p, side], far_box.at[p, side], fs.at[p, side], fr.at[p, side],
            {"tp": t_right if side == 0 else t_left},
        )

    def near_send(p, direction, side):
        return remote(
            near_stage.at[p, direction, side], near_box.at[p, direction, side],
            ns.at[p, direction, side], nr.at[p, direction, side],
            {"tp": t_right if direction == 0 else t_left},
        )

    for p in range(PIECES):
        z_step(p, 0)
    load_w.wait()
    for copy in own_copies:
        copy.wait()
    for h in range(1, 5):
        z_step(0, h)
    for p in range(PIECES):
        more = p + 1 < PIECES
        value = product(p, 2)
        for side in range(2):
            far_stage[p, side] = value[:, half(side)].astype(BF16)
            far_send(p, side).start()
        if more:
            z_step(p + 1, 1)
        right = product(p, 1)
        near_stage[p, 0, 1] = right[:, half(1)].astype(BF16)
        near_send(p, 0, 1).start()
        left = product(p, 3)
        near_stage[p, 1, 0] = left[:, half(0)].astype(BF16)
        near_send(p, 1, 0).start()
        if more:
            z_step(p + 1, 2)
        far_send(p, 0).wait_recv()
        near_stage[p, 0, 0] = (right[:, half(0)] + far_box[p, 0].astype(F32)).astype(BF16)
        near_send(p, 0, 0).start()
        far_send(p, 1).wait_recv()
        near_stage[p, 1, 1] = (left[:, half(1)] + far_box[p, 1].astype(F32)).astype(BF16)
        near_send(p, 1, 1).start()
        if more:
            z_step(p + 1, 3)
        mine = product(p, 0)
        if more:
            z_step(p + 1, 4)
        for side in range(2):
            near_send(p, 0, side).wait_recv()
            near_send(p, 1, side).wait_recv()
            summed = mine[:, half(side)] + near_box[p, 0, side].astype(F32)
            summed = summed + near_box[p, 1, side].astype(F32)
            out[:, p, :, half(side)] = summed.reshape(2, PROWS, OUTW // 2).astype(BF16)
    for p in range(PIECES):
        for direction in range(2):
            for h in range(z_hops(p, direction)):
                z_send(p, direction, h).wait_send()
            far_send(p, direction).wait_send()
            for side in range(2):
                near_send(p, direction, side).wait_send()


def project_out(attended, w):
    half = OUTW // 2
    out = pl.pallas_call(
        out_kernel,
        out_shape=jax.ShapeDtypeStruct((2, PIECES, PROWS, OUTW), BF16),
        in_specs=[ANY, HBM],
        out_specs=VM,
        scratch_shapes=[
            pltpu.VMEM((FEAT, OUTW), BF16),
            pltpu.VMEM((NZ, PIECES, PROWS, FEAT), BF16),
            pltpu.VMEM((PIECES, 2, 2 * PROWS, half), BF16),
            pltpu.VMEM((PIECES, 2, 2, 2 * PROWS, half), BF16),
            pltpu.VMEM((PIECES, 2, 2 * PROWS, half), BF16),
            pltpu.VMEM((PIECES, 2, 2, 2 * PROWS, half), BF16),
            DMA((1 + PIECES,)),
            DMA((PIECES, 2, 4)), DMA((PIECES, 2, 4)),
            DMA((PIECES, 2)), DMA((PIECES, 2)),
            DMA((PIECES, 2, 2)), DMA((PIECES, 2, 2)),
        ],
        compiler_params=pltpu.CompilerParams(
            collective_id=2, has_side_effects=True, vmem_limit_bytes=62 << 20
        ),
        name="project_out",
    )(attended.reshape(PIECES, PROWS, FEAT), w)
    return out.reshape(2 * ROWS, OUTW)


def rope_frequencies():
    base = THETA ** (-2.0 * np.arange(HEAD // 2, dtype=np.float64) / HEAD)
    wavelen = 2.0 * np.pi / base
    smooth = (8192.0 / wavelen - 1.0) / 3.0
    blended = (1.0 - smooth) * base / 8.0 + smooth * base
    scaled = np.where(wavelen > 8192.0, base / 8.0, np.where(wavelen < 2048.0, base, blended))
    return jnp.asarray(np.tile(scaled, 2)[None, :], F32)


def on_device(hidden, norm_gain, query_key_value_weight, w_out, doc_ids, block_order):
    weights = query_key_value_weight.reshape(FEAT, COLS)
    gain = norm_gain.reshape(NZ * FEAT // 128, 128)
    docs = doc_ids.reshape(NZ * FEAT // 128, 128)
    q, kv_all = project(block_order, rope_frequencies(), gain, hidden, weights)
    attended = attend(block_order, docs, q, kv_all)
    return project_out(attended, w_out)


def solution(mesh):
    return jax.shard_map(
        on_device,
        mesh=mesh,
        in_specs=(P(("blk", "uly"), None), P(), P("uly", "tp", None), P("tp", "uly"), P(), P()),
        out_specs=P(("blk", "tp"), "uly"),
        check_vma=False,
    )
```

```python
import math

import jax
import jax.numpy as jnp
import numpy as np
from jax import lax
from jax.experimental import pallas as pl
from jax.experimental.pallas import tpu as pltpu
from jax.sharding import PartitionSpec as P

HEAD = 128
HEADS = 8
BLOCK = 512
THETA = 500000.0
NEG_BIG = -1e30
NZ = 8
NT = 4
ROWS = 128
SUB = ROWS // NT
FEAT = 1024
COLS = (HEADS + 2) * HEAD
MESH = pl.DeviceIdType.MESH
F32 = jnp.float32
BF16 = jnp.bfloat16
FAR_FIRST = (4, 3, 5, 2, 6, 1, 7)
QSCALE = math.log2(math.e) / math.sqrt(HEAD)


def remote(src, dst, send_sem, recv_sem, device):
    return pltpu.make_async_remote_copy(
        src_ref=src,
        dst_ref=dst,
        send_sem=send_sem,
        recv_sem=recv_sem,
        device_id=device,
        device_id_type=MESH,
    )


def greet(devices):
    barrier = pltpu.get_barrier_semaphore()
    for device in devices:
        pl.semaphore_signal(barrier, inc=1, device_id=device, device_id_type=MESH)
    pl.semaphore_wait(barrier, len(devices))


def dot32(a, b):
    return jnp.dot(a, b, preferred_element_type=F32)


KCOL = HEADS * HEAD
PIECE_COLS = (slice(KCOL, KCOL + HEAD), slice(KCOL + HEAD, COLS), slice(0, KCOL // 2), slice(KCOL // 2, KCOL))
QUARTERED = 5
Z_STEPS = (0, -1, 1, -2, 2, -3, 3, -4)


def proj_kernel(
    order, freq, gain, hid, w, q_out, kv_all,
    hloc, wloc, wg, g32, xbuf, own, far, pairs, kv, rope, row_scale,
    kv_stage, kv_inbox, q_stage, q_inbox,
    lsem, zs, zr, ys, yr, fs, fr, ks, kr, qs, qr,
    gzs, gzr, gxs, gxr, gfs, gfr, gss, gsr,
):
    b = lax.axis_index("blk")
    u = lax.axis_index("uly")
    t = lax.axis_index("tp")
    t_right, t_left, across = lax.rem(t + 1, NT), lax.rem(t + 3, NT), lax.rem(t + 2, NT)
    u_right, u_left = lax.rem(u + 1, NZ), lax.rem(u + NZ - 1, NZ)
    b_right, b_left, b_across = lax.rem(b + 2, 8), lax.rem(b + 6, 8), lax.rem(b + 4, 8)
    sibling = b + 1 - 2 * lax.rem(b, 2)
    load_w = pltpu.make_async_copy(w, wloc, lsem.at[0])
    load_h = pltpu.make_async_copy(hid, hloc, lsem.at[1])
    load_w.start()
    load_h.start()
    greet(
        [{"uly": lax.rem(u + k, NZ)} for k in range(1, NZ)]
        + [{"tp": t_right}, {"tp": t_left}, {"blk": b_right}, {"blk": b_left}, {"blk": sibling}]
    )

    def part(owner):
        return pl.ds(pl.multiple_of(owner * SUB, SUB), SUB)

    def feats(owner):
        return pl.ds(pl.multiple_of(owner * FEAT, FEAT), FEAT)

    over_z = []
    for i, k in enumerate(FAR_FIRST):
        v = lax.rem(u + NZ - k, NZ)
        if i < QUARTERED:
            src, dst = hid.at[part(t), feats(v)], xbuf.at[i, part(t)]
        else:
            src, dst = hid.at[:, feats(v)], xbuf.at[i]
        copy = remote(src, dst, zs.at[i], zr.at[i], {"uly": v})
        copy.start()
        over_z.append(copy)

    g32[...] = gain[...].astype(F32)
    load_w.wait()

    def fold(c, carry):
        r = pl.ds(pl.multiple_of(c * 128, 128), 128)
        column = jnp.broadcast_to(g32[pl.ds(u * NZ + c, 1), :], (128, 128)).T
        for n in range(COLS // 128):
            lanes = slice(n * 128, (n + 1) * 128)
            wg[r, lanes] = (wloc[r, lanes].astype(F32) * column).astype(BF16)
        return carry

    lax.fori_loop(0, FEAT // 128, fold, 0)
    load_h.wait()

    def square(c, acc):
        x = hloc[:, pl.ds(pl.multiple_of(c * 128, 128), 128)].astype(F32)
        return acc + x * x

    total = lax.fori_loop(0, NZ * FEAT // 128, square, jnp.zeros((ROWS, 128), F32))
    mean = jnp.sum(total, axis=1, keepdims=True) / (NZ * FEAT)
    row_scale[...] = jnp.broadcast_to(lax.rsqrt(mean + 1e-05), (ROWS, HEAD))
    shard_id = b * NZ + u
    block = shard_id // (BLOCK // ROWS)
    first = order[block] * BLOCK + lax.rem(shard_id, BLOCK // ROWS) * ROWS
    position = (lax.broadcasted_iota(jnp.int32, (ROWS, HEAD), 0) + first).astype(F32)
    angles = position * freq[...]
    left_half = lax.broadcasted_iota(jnp.int32, (ROWS, HEAD), 1) < HEAD // 2
    sines = jnp.sin(angles)
    rope[0] = jnp.cos(angles)
    rope[1] = jnp.where(left_half, -sines, sines)

    def chunk_from(i, source, direction):
        return remote(
            xbuf.at[i, part(source)], xbuf.at[i, part(source)],
            ys.at[i, direction], yr.at[i, direction],
            {"tp": t_right if direction == 0 else t_left},
        )

    def pass_on(i):
        source, target = (t_left, t_right) if i % 2 == 0 else (t_right, t_left)
        return remote(
            xbuf.at[i, part(source)], xbuf.at[i, part(source)], fs.at[i], fr.at[i], {"tp": target}
        )

    def kv_copy(step, direction, piece):
        return remote(
            kv_stage.at[direction, step, piece], kv_inbox.at[direction, step, piece],
            ks.at[direction, step, piece], kr.at[direction, step, piece],
            {"uly": u_right if direction == 0 else u_left},
        )

    def q_copy(step, direction, piece):
        return remote(
            q_stage.at[direction, step, piece], q_inbox.at[direction, step, piece],
            qs.at[direction, step, piece], qr.at[direction, step, piece],
            {"uly": u_right if direction == 0 else u_left},
        )

    def mine(step, direction, cols):
        if step == 0:
            return far[:, cols]
        return pairs[step - 1, direction * ROWS : (direction + 1) * ROWS, cols]

    def send_kv(step, direction, piece):
        value = mine(step, direction, PIECE_COLS[piece])
        if step > 1 or (step == 1 and piece == direction):
            kv_copy(step - 1, direction, piece).wait_recv()
            value = value + kv_inbox[direction, step - 1, piece].astype(F32)
        kv_stage[direction, step, piece] = value.astype(BF16)
        kv_copy(step, direction, piece).start()

    def send_q(step, direction, piece):
        value = mine(step, direction, PIECE_COLS[2 + piece])
        if step > 1 or (step == 1 and piece == direction):
            q_copy(step - 1, direction, piece).wait_recv()
            value = value + q_inbox[direction, step - 1, piece].astype(F32)
        q_stage[direction, step, piece] = value.astype(BF16)
        q_copy(step, direction, piece).start()

    def far_product():
        far[...] = dot32(xbuf[0], wg[...])
        for direction in range(2):
            send_kv(0, direction, direction)

    def pair_product(j):
        x = xbuf[2 * j - 1 : 2 * j + 1].reshape(2 * ROWS, FEAT)
        pairs[j - 1] = dot32(x, wg[...])

    for tick in range(QUARTERED + 4):
        if tick < QUARTERED:
            over_z[tick].wait_recv()
            chunk_from(tick, t, 0).start()
            chunk_from(tick, t, 1).start()
        if tick == 0:
            own[...] = dot32(hloc[:, feats(u)], wg[...])
        i = tick - 2
        if 0 <= i < QUARTERED:
            chunk_from(i, t_left, 0).wait_recv()
            chunk_from(i, t_right, 1).wait_recv()
            pass_on(i).start()
        i = tick - 4
        if 0 <= i < QUARTERED:
            remote(
                xbuf.at[i, part(across)], xbuf.at[i, part(across)], fs.at[i], fr.at[i],
                {"tp": t_right},
            ).wait_recv()
            if i == 0:
                far_product()
            elif i % 2 == 0:
                pair_product(i // 2)
            if i == 2:
                for direction in range(2):
                    send_kv(1, direction, 1 - direction)
                    send_kv(1, direction, direction)
                for direction in range(2):
                    send_q(0, direction, direction)
                for direction in range(2):
                    send_q(1, direction, 1 - direction)
    for direction in range(2):
        for piece in range(2):
            send_kv(2, direction, piece)
    over_z[QUARTERED].wait_recv()
    over_z[QUARTERED + 1].wait_recv()
    pair_product(3)
    for direction in range(2):
        for piece in range(2):
            send_kv(3, direction, piece)
    for direction in range(2):
        send_q(1, direction, direction)

    def rotated(x):
        return x * rope[0] + pltpu.roll(x, HEAD // 2, 1) * rope[1]

    for piece in range(2):
        kv_copy(3, 0, piece).wait_recv()
        kv_copy(3, 1, piece).wait_recv()
        x = own[:, PIECE_COLS[piece]]
        x = x + kv_inbox[0, 3, piece].astype(F32)
        x = (x + kv_inbox[1, 3, piece].astype(F32)) * row_scale[...]
        if piece == 0:
            x = rotated(x)
        kv[:, piece * HEAD : (piece + 1) * HEAD] = x.astype(BF16)

    def z_of(i):
        return lax.rem(u + Z_STEPS[i] + NZ, NZ)

    def shard(owner, i):
        return kv_all.at[owner * NZ + z_of(i)]

    def held(i):
        return kv if i == 0 else shard(b, i)

    def z_copy(i, src, dst):
        to = u_right if Z_STEPS[i] < 0 else u_left
        return remote(src, dst, gzs.at[i], gzr.at[i], {"uly": to})

    def x_send(i, direction):
        return remote(
            held(i), shard(b, i), gxs.at[i, direction], gxr.at[i, direction],
            {"blk": b_right if direction == 0 else b_left},
        )

    def x_wait(i, direction):
        source = b_left if direction == 0 else b_right
        return remote(
            shard(source, i), shard(source, i), gxs.at[i, direction], gxr.at[i, direction],
            {"blk": b_right},
        )

    def x_pass(i):
        source, target = (b_left, b_right) if i % 2 == 0 else (b_right, b_left)
        return remote(shard(source, i), shard(source, i), gfs.at[i], gfr.at[i], {"blk": target})

    def side(i, m):
        owner = (b, b_left, b_right, b_across)[m]
        src = held(i) if m == 0 else shard(owner, i)
        return remote(src, shard(owner, i), gss.at[i, m], gsr.at[i, m], {"blk": sibling})

    def side_wait(i, m):
        owner = lax.rem(sibling + (0, 6, 2, 4)[m], 8)
        return remote(shard(owner, i), shard(owner, i), gss.at[i, m], gsr.at[i, m], {"blk": sibling})

    z_sends = []

    def start_z(step, src_i):
        copy = z_copy(Z_STEPS.index(step), held(src_i), shard(b, src_i))
        copy.start()
        z_sends.append(copy)

    place_own = pltpu.make_async_copy(kv, kv_all.at[b * NZ + u], lsem.at[2])

    def gather_tick(tick):
        i = tick
        if i < NZ:
            step = Z_STEPS[i]
            if i == 0:
                start_z(-1, 0)
                start_z(1, 0)
                place_own.start()
            else:
                z_copy(i, shard(b, i), shard(b, i)).wait_recv()
                if -4 < step < 0:
                    start_z(step - 1, i)
                if 0 < step < 3:
                    start_z(step + 1, i)
            x_send(i, 0).start()
            x_send(i, 1).start()
            side(i, 0).start()
        i = tick - 2
        if 0 <= i < NZ:
            x_wait(i, 0).wait_recv()
            x_wait(i, 1).wait_recv()
            x_pass(i).start()
            side(i, 1).start()
            side(i, 2).start()
        i = tick - 4
        if 0 <= i < NZ:
            remote(
                shard(b_across, i), shard(b_across, i), gfs.at[i], gfr.at[i], {"blk": b_right}
            ).wait_recv()
            side(i, 3).start()

    def finish_q(piece):
        q_copy(3, 0, piece).wait_recv()
        q_copy(3, 1, piece).wait_recv()
        cols = PIECE_COLS[2 + piece]
        x = own[:, cols] + q_inbox[0, 3, piece].astype(F32)
        own[:, cols] = (x + q_inbox[1, 3, piece].astype(F32)) * (row_scale[:, :1] * QSCALE)
        for h in range(piece * HEADS // 2, (piece + 1) * HEADS // 2):
            x = rotated(own[:, h * HEAD : (h + 1) * HEAD])
            q_out[h * ROWS : (h + 1) * ROWS, :] = x.astype(BF16)

    gather_tick(0)
    for direction in range(2):
        send_q(2, direction, 1 - direction)
    gather_tick(1)
    gather_tick(2)
    for direction in range(2):
        send_q(2, direction, direction)
    gather_tick(3)
    gather_tick(4)
    for direction in range(2):
        send_q(3, direction, 1 - direction)
    gather_tick(5)
    gather_tick(6)
    for direction in range(2):
        send_q(3, direction, direction)
    gather_tick(7)
    gather_tick(8)
    finish_q(0)
    gather_tick(9)
    finish_q(1)
    gather_tick(10)
    gather_tick(11)
    place_own.wait()
    for i in range(NZ):
        for m in range(4):
            side_wait(i, m).wait_recv()

    for copy in over_z:
        copy.wait_send()
    for i in range(QUARTERED):
        chunk_from(i, t, 0).wait_send()
        chunk_from(i, t, 1).wait_send()
        pass_on(i).wait_send()
    for direction in range(2):
        for step in range(4):
            for piece in range(2):
                if step > 0 or piece == direction:
                    kv_copy(step, direction, piece).wait_send()
                    q_copy(step, direction, piece).wait_send()
    for copy in z_sends:
        copy.wait_send()
    for i in range(NZ):
        x_send(i, 0).wait_send()
        x_send(i, 1).wait_send()
        x_pass(i).wait_send()
        for m in range(4):
            side(i, m).wait_send()


ANY = pl.BlockSpec(memory_space=pl.ANY)
VM = pl.BlockSpec(memory_space=pltpu.VMEM)
DMA = pltpu.SemaphoreType.DMA


HBM = pl.BlockSpec(memory_space=pltpu.HBM)
SM = pl.BlockSpec(memory_space=pltpu.SMEM)


def project(order, freq, gain, hidden, weights):
    n = NZ - 1
    return pl.pallas_call(
        proj_kernel,
        out_shape=(
            jax.ShapeDtypeStruct((HEADS * ROWS, HEAD), BF16),
            jax.ShapeDtypeStruct((8 * NZ, ROWS, 2 * HEAD), BF16),
        ),
        in_specs=[SM, VM, VM, HBM, HBM],
        out_specs=(VM, VM),
        scratch_shapes=[
            pltpu.VMEM((ROWS, NZ * FEAT), BF16),
            pltpu.VMEM((FEAT, COLS), BF16),
            pltpu.VMEM((FEAT, COLS), BF16),
            pltpu.VMEM((NZ * FEAT // 128, 128), F32),
            pltpu.VMEM((n, ROWS, FEAT), BF16),
            pltpu.VMEM((ROWS, COLS), F32),
            pltpu.VMEM((ROWS, COLS), F32),
            pltpu.VMEM((3, 2 * ROWS, COLS), F32),
            pltpu.VMEM((ROWS, 2 * HEAD), BF16),
            pltpu.VMEM((2, ROWS, HEAD), F32),
            pltpu.VMEM((ROWS, HEAD), F32),
            pltpu.VMEM((2, 4, 2, ROWS, HEAD), BF16),
            pltpu.VMEM((2, 4, 2, ROWS, HEAD), BF16),
            pltpu.VMEM((2, 4, 2, ROWS, KCOL // 2), BF16),
            pltpu.VMEM((2, 4, 2, ROWS, KCOL // 2), BF16),
            DMA((3,)),
            DMA((n,)), DMA((n,)),
            DMA((n, 2)), DMA((n, 2)),
            DMA((n,)), DMA((n,)),
            DMA((2, 4, 2)), DMA((2, 4, 2)),
            DMA((2, 4, 2)), DMA((2, 4, 2)),
            DMA((NZ,)), DMA((NZ,)),
            DMA((NZ, 2)), DMA((NZ, 2)),
            DMA((NZ,)), DMA((NZ,)),
            DMA((NZ, 4)), DMA((NZ, 4)),
        ],
        compiler_params=pltpu.CompilerParams(
            collective_id=0, has_side_effects=True, vmem_limit_bytes=62 << 20
        ),
        name="project",
    )(order, freq, gain, hidden, weights)


def attend_kernel(order, docs, q, kv, out, inverse, m_ref, l_ref, acc):
    per = BLOCK // ROWS
    shard = lax.axis_index("blk") * NZ + lax.axis_index("uly")
    q_block = order[shard // per] * per + lax.rem(shard, per)
    for r in range(16):
        inverse[order[r]] = r
    segment = docs[pl.ds(q_block, 1), :]
    starts = jnp.zeros((1, ROWS), jnp.int32)
    for n in range(1, 16):
        before = jnp.sum((docs[...] < n).astype(jnp.int32))
        starts = jnp.where(segment == n, before, starts)
    count = q_block - jnp.min(starts) // ROWS + 1
    wide = HEADS * ROWS
    m_ref[...] = jnp.full((1, wide), NEG_BIG, F32)
    l_ref[...] = jnp.zeros((1, wide), F32)
    acc[...] = jnp.zeros((HEAD, wide), F32)
    lane = lax.broadcasted_iota(jnp.int32, (128, ROWS), 1)
    row = lax.broadcasted_iota(jnp.int32, (128, ROWS), 0)
    causal = row <= lane
    starts = jnp.broadcast_to(starts, (128, ROWS))

    def step(i, carry):
        k_block = q_block - i
        at = inverse[k_block // per] * per + lax.rem(k_block, per)
        k = kv[at, :, :HEAD]
        v = kv[at, :, HEAD:]
        scores = lax.dot_general(
            k, q[...], (((1,), (1,)), ((), ())), preferred_element_type=F32
        )
        allowed = (row + k_block * 128 >= starts) & (causal | (i > 0))
        bias = jnp.where(allowed, 0.0, NEG_BIG)
        scores = scores + jnp.concatenate([bias] * HEADS, axis=1)
        m_old = m_ref[...]
        m_new = jnp.maximum(m_old, jnp.max(scores, axis=0, keepdims=True))
        weights = jnp.exp2(scores - m_new)
        factor = jnp.exp2(m_old - m_new)
        m_ref[...] = m_new
        l_ref[...] = l_ref[...] * factor + jnp.sum(weights, axis=0, keepdims=True)
        mixed = lax.dot_general(
            v, weights.astype(BF16), (((0,), (0,)), ((), ())), preferred_element_type=F32
        )
        acc[...] = acc[...] * factor + mixed
        return carry

    lax.fori_loop(0, count, step, 0)
    result = acc[...] / l_ref[...]
    for h in range(HEADS):
        part = result[:, h * ROWS : (h + 1) * ROWS]
        out[:, h * HEAD : (h + 1) * HEAD] = part.T.astype(BF16)


def attend(order, docs, q, kv):
    wide = HEADS * ROWS
    return pl.pallas_call(
        attend_kernel,
        out_shape=jax.ShapeDtypeStruct((ROWS, HEADS * HEAD), BF16),
        in_specs=[SM, VM, VM, VM],
        out_specs=VM,
        scratch_shapes=[
            pltpu.SMEM((16,), jnp.int32),
            pltpu.VMEM((1, wide), F32),
            pltpu.VMEM((1, wide), F32),
            pltpu.VMEM((HEAD, wide), F32),
        ],
        compiler_params=pltpu.CompilerParams(vmem_limit_bytes=60 << 20),
        name="attend",
    )(order, docs, q, kv)


PIECES = 2
PROWS = ROWS // PIECES
OUTW = 1024


def out_kernel(att, w, out, wloc, abuf, far_stage, near_stage, far_box, near_box,
               lsem, zs, zr, fs, fr, ns, nr):
    u = lax.axis_index("uly")
    t = lax.axis_index("tp")
    t_right, t_left = lax.rem(t + 1, NT), lax.rem(t + NT - 1, NT)
    u_right, u_left = lax.rem(u + 1, NZ), lax.rem(u + NZ - 1, NZ)
    load_w = pltpu.make_async_copy(w, wloc, lsem.at[0])
    load_w.start()
    own_copies = []
    for p in range(PIECES):
        copy = pltpu.make_async_copy(att.at[p], abuf.at[u, p], lsem.at[1 + p])
        copy.start()
        own_copies.append(copy)
    greet([{"uly": u_right}, {"uly": u_left}, {"tp": t_right}, {"tp": t_left}])

    def z_hops(p, direction):
        return 4 if (p + direction) % 2 == 0 else 3

    def chunk(direction, h):
        return lax.rem(u + NZ + (-h if direction == 0 else h), NZ)

    def z_copy(p, direction, h, source):
        src = att.at[p] if h == 0 else abuf.at[source, p]
        return remote(
            src, abuf.at[source, p], zs.at[p, direction, h], zr.at[p, direction, h],
            {"uly": u_right if direction == 0 else u_left},
        )

    def z_send(p, direction, h):
        return z_copy(p, direction, h, chunk(direction, h))

    def z_wait(p, direction, h):
        source = chunk(direction, h + 1)
        return remote(
            abuf.at[source, p], abuf.at[source, p], zs.at[p, direction, h],
            zr.at[p, direction, h], {"uly": u_right},
        )

    def z_step(p, h):
        for direction in range(2):
            hops = z_hops(p, direction)
            if h > 0 and h <= hops:
                z_wait(p, direction, h - 1).wait_recv()
            if h < hops:
                z_send(p, direction, h).start()

    def product(p, rel):
        d = lax.rem(t + rel, NT)
        x = abuf[pl.ds(2 * d, 2), p].reshape(2 * PROWS, FEAT)
        return dot32(x, wloc[...])

    def half(side):
        return slice(side * (OUTW // 2), (side + 1) * (OUTW // 2))

    def far_send(p, side):
        return remote(
            far_stage.at[p, side], far_box.at[p, side], fs.at[p, side], fr.at[p, side],
            {"tp": t_right if side == 0 else t_left},
        )

    def near_send(p, direction, side):
        return remote(
            near_stage.at[p, direction, side], near_box.at[p, direction, side],
            ns.at[p, direction, side], nr.at[p, direction, side],
            {"tp": t_right if direction == 0 else t_left},
        )

    for p in range(PIECES):
        z_step(p, 0)
    load_w.wait()
    for copy in own_copies:
        copy.wait()
    for h in range(1, 5):
        z_step(0, h)
    for p in range(PIECES):
        more = p + 1 < PIECES
        value = product(p, 2)
        for side in range(2):
            far_stage[p, side] = value[:, half(side)].astype(BF16)
            far_send(p, side).start()
        if more:
            z_step(p + 1, 1)
        right = product(p, 1)
        near_stage[p, 0, 1] = right[:, half(1)].astype(BF16)
        near_send(p, 0, 1).start()
        left = product(p, 3)
        near_stage[p, 1, 0] = left[:, half(0)].astype(BF16)
        near_send(p, 1, 0).start()
        if more:
            z_step(p + 1, 2)
        far_send(p, 0).wait_recv()
        near_stage[p, 0, 0] = (right[:, half(0)] + far_box[p, 0].astype(F32)).astype(BF16)
        near_send(p, 0, 0).start()
        far_send(p, 1).wait_recv()
        near_stage[p, 1, 1] = (left[:, half(1)] + far_box[p, 1].astype(F32)).astype(BF16)
        near_send(p, 1, 1).start()
        if more:
            z_step(p + 1, 3)
        mine = product(p, 0)
        if more:
            z_step(p + 1, 4)
        for side in range(2):
            near_send(p, 0, side).wait_recv()
            near_send(p, 1, side).wait_recv()
            summed = mine[:, half(side)] + near_box[p, 0, side].astype(F32)
            summed = summed + near_box[p, 1, side].astype(F32)
            out[:, p, :, half(side)] = summed.reshape(2, PROWS, OUTW // 2).astype(BF16)
    for p in range(PIECES):
        for direction in range(2):
            for h in range(z_hops(p, direction)):
                z_send(p, direction, h).wait_send()
            far_send(p, direction).wait_send()
            for side in range(2):
                near_send(p, direction, side).wait_send()


def project_out(attended, w):
    half = OUTW // 2
    out = pl.pallas_call(
        out_kernel,
        out_shape=jax.ShapeDtypeStruct((2, PIECES, PROWS, OUTW), BF16),
        in_specs=[ANY, HBM],
        out_specs=VM,
        scratch_shapes=[
            pltpu.VMEM((FEAT, OUTW), BF16),
            pltpu.VMEM((NZ, PIECES, PROWS, FEAT), BF16),
            pltpu.VMEM((PIECES, 2, 2 * PROWS, half), BF16),
            pltpu.VMEM((PIECES, 2, 2, 2 * PROWS, half), BF16),
            pltpu.VMEM((PIECES, 2, 2 * PROWS, half), BF16),
            pltpu.VMEM((PIECES, 2, 2, 2 * PROWS, half), BF16),
            DMA((1 + PIECES,)),
            DMA((PIECES, 2, 4)), DMA((PIECES, 2, 4)),
            DMA((PIECES, 2)), DMA((PIECES, 2)),
            DMA((PIECES, 2, 2)), DMA((PIECES, 2, 2)),
        ],
        compiler_params=pltpu.CompilerParams(
            collective_id=2, has_side_effects=True, vmem_limit_bytes=62 << 20
        ),
        name="project_out",
    )(attended.reshape(PIECES, PROWS, FEAT), w)
    return out.reshape(2 * ROWS, OUTW)


def rope_frequencies():
    base = THETA ** (-2.0 * np.arange(HEAD // 2, dtype=np.float64) / HEAD)
    wavelen = 2.0 * np.pi / base
    smooth = (8192.0 / wavelen - 1.0) / 3.0
    blended = (1.0 - smooth) * base / 8.0 + smooth * base
    scaled = np.where(wavelen > 8192.0, base / 8.0, np.where(wavelen < 2048.0, base, blended))
    return jnp.asarray(np.tile(scaled, 2)[None, :], F32)


def on_device(hidden, norm_gain, query_key_value_weight, w_out, doc_ids, block_order):
    weights = query_key_value_weight.reshape(FEAT, COLS)
    gain = norm_gain.reshape(NZ * FEAT // 128, 128)
    docs = doc_ids.reshape(NZ * FEAT // 128, 128)
    q, kv_all = project(block_order, rope_frequencies(), gain, hidden, weights)
    attended = attend(block_order, docs, q, kv_all)
    return project_out(attended, w_out)


def solution(mesh):
    return jax.shard_map(
        on_device,
        mesh=mesh,
        in_specs=(P(("blk", "uly"), None), P(), P("uly", "tp", None), P("tp", "uly"), P(), P()),
        out_specs=P(("blk", "tp"), "uly"),
        check_vma=False,
    )
```

```python
import math

import jax
import jax.numpy as jnp
import numpy as np
from jax import lax
from jax.experimental import pallas as pl
from jax.experimental.pallas import tpu as pltpu
from jax.sharding import PartitionSpec as P

HEAD = 128
HEADS = 8
BLOCK = 512
THETA = 500000.0
NEG_BIG = -1e30
NZ = 8
NT = 4
ROWS = 128
SUB = ROWS // NT
FEAT = 1024
COLS = (HEADS + 2) * HEAD
MESH = pl.DeviceIdType.MESH
F32 = jnp.float32
BF16 = jnp.bfloat16
FAR_FIRST = (4, 3, 5, 2, 6, 1, 7)
QSCALE = math.log2(math.e) / math.sqrt(HEAD)


def remote(src, dst, send_sem, recv_sem, device):
    return pltpu.make_async_remote_copy(
        src_ref=src,
        dst_ref=dst,
        send_sem=send_sem,
        recv_sem=recv_sem,
        device_id=device,
        device_id_type=MESH,
    )


def greet(devices):
    barrier = pltpu.get_barrier_semaphore()
    for device in devices:
        pl.semaphore_signal(barrier, inc=1, device_id=device, device_id_type=MESH)
    pl.semaphore_wait(barrier, len(devices))


def dot32(a, b):
    return jnp.dot(a, b, preferred_element_type=F32)


KCOL = HEADS * HEAD
PIECE_COLS = (slice(KCOL, KCOL + HEAD), slice(KCOL + HEAD, COLS), slice(0, KCOL // 2), slice(KCOL // 2, KCOL))
QUARTERED = 5
Z_STEPS = (0, -1, 1, -2, 2, -3, 3, -4)


def proj_kernel(
    order, freq, gain, hid, w, q_out, kv_all,
    hloc, wloc, wg, g32, xbuf, own, far, pairs, kv, rope, row_scale,
    kv_stage, kv_inbox, q_stage, q_inbox,
    lsem, zs, zr, ys, yr, fs, fr, ks, kr, qs, qr,
    gzs, gzr, gxs, gxr, gfs, gfr, gss, gsr,
):
    b = lax.axis_index("blk")
    u = lax.axis_index("uly")
    t = lax.axis_index("tp")
    t_right, t_left, across = lax.rem(t + 1, NT), lax.rem(t + 3, NT), lax.rem(t + 2, NT)
    u_right, u_left = lax.rem(u + 1, NZ), lax.rem(u + NZ - 1, NZ)
    b_right, b_left, b_across = lax.rem(b + 2, 8), lax.rem(b + 6, 8), lax.rem(b + 4, 8)
    sibling = b + 1 - 2 * lax.rem(b, 2)
    load_w = pltpu.make_async_copy(w, wloc, lsem.at[0])
    load_h = pltpu.make_async_copy(hid, hloc, lsem.at[1])
    load_w.start()
    load_h.start()
    greet(
        [{"uly": lax.rem(u + k, NZ)} for k in range(1, NZ)]
        + [{"tp": t_right}, {"tp": t_left}, {"blk": b_right}, {"blk": b_left}, {"blk": sibling}]
    )

    def part(owner):
        return pl.ds(pl.multiple_of(owner * SUB, SUB), SUB)

    def feats(owner):
        return pl.ds(pl.multiple_of(owner * FEAT, FEAT), FEAT)

    over_z = []
    for i, k in enumerate(FAR_FIRST):
        v = lax.rem(u + NZ - k, NZ)
        if i < QUARTERED:
            src, dst = hid.at[part(t), feats(v)], xbuf.at[i, part(t)]
        else:
            src, dst = hid.at[:, feats(v)], xbuf.at[i]
        copy = remote(src, dst, zs.at[i], zr.at[i], {"uly": v})
        copy.start()
        over_z.append(copy)

    g32[...] = gain[...].astype(F32)
    load_w.wait()

    def fold(c, carry):
        r = pl.ds(pl.multiple_of(c * 128, 128), 128)
        column = jnp.broadcast_to(g32[pl.ds(u * NZ + c, 1), :], (128, 128)).T
        for n in range(COLS // 128):
            lanes = slice(n * 128, (n + 1) * 128)
            wg[r, lanes] = (wloc[r, lanes].astype(F32) * column).astype(BF16)
        return carry

    lax.fori_loop(0, FEAT // 128, fold, 0)
    load_h.wait()

    def square(c, acc):
        x = hloc[:, pl.ds(pl.multiple_of(c * 128, 128), 128)].astype(F32)
        return acc + x * x

    total = lax.fori_loop(0, NZ * FEAT // 128, square, jnp.zeros((ROWS, 128), F32))
    mean = jnp.sum(total, axis=1, keepdims=True) / (NZ * FEAT)
    row_scale[...] = jnp.broadcast_to(lax.rsqrt(mean + 1e-05), (ROWS, HEAD))
    shard_id = b * NZ + u
    block = shard_id // (BLOCK // ROWS)
    first = order[block] * BLOCK + lax.rem(shard_id, BLOCK // ROWS) * ROWS
    position = (lax.broadcasted_iota(jnp.int32, (ROWS, HEAD), 0) + first).astype(F32)
    angles = position * freq[...]
    left_half = lax.broadcasted_iota(jnp.int32, (ROWS, HEAD), 1) < HEAD // 2
    sines = jnp.sin(angles)
    rope[0] = jnp.cos(angles)
    rope[1] = jnp.where(left_half, -sines, sines)

    def chunk_from(i, source, direction):
        return remote(
            xbuf.at[i, part(source)], xbuf.at[i, part(source)],
            ys.at[i, direction], yr.at[i, direction],
            {"tp": t_right if direction == 0 else t_left},
        )

    def pass_on(i):
        source, target = (t_left, t_right) if i % 2 == 0 else (t_right, t_left)
        return remote(
            xbuf.at[i, part(source)], xbuf.at[i, part(source)], fs.at[i], fr.at[i], {"tp": target}
        )

    def kv_copy(step, direction, piece):
        return remote(
            kv_stage.at[direction, step, piece], kv_inbox.at[direction, step, piece],
            ks.at[direction, step, piece], kr.at[direction, step, piece],
            {"uly": u_right if direction == 0 else u_left},
        )

    def q_copy(step, direction, piece):
        return remote(
            q_stage.at[direction, step, piece], q_inbox.at[direction, step, piece],
            qs.at[direction, step, piece], qr.at[direction, step, piece],
            {"uly": u_right if direction == 0 else u_left},
        )

    def mine(step, direction, cols):
        if step == 0:
            return far[:, cols]
        return pairs[step - 1, direction * ROWS : (direction + 1) * ROWS, cols]

    def send_kv(step, direction, piece):
        value = mine(step, direction, PIECE_COLS[piece])
        if step > 1 or (step == 1 and piece == direction):
            kv_copy(step - 1, direction, piece).wait_recv()
            value = value + kv_inbox[direction, step - 1, piece].astype(F32)
        kv_stage[direction, step, piece] = value.astype(BF16)
        kv_copy(step, direction, piece).start()

    def send_q(step, direction, piece):
        value = mine(step, direction, PIECE_COLS[2 + piece])
        if step > 1 or (step == 1 and piece == direction):
            q_copy(step - 1, direction, piece).wait_recv()
            value = value + q_inbox[direction, step - 1, piece].astype(F32)
        q_stage[direction, step, piece] = value.astype(BF16)
        q_copy(step, direction, piece).start()

    def far_product():
        far[...] = dot32(xbuf[0], wg[...])
        for direction in range(2):
            send_kv(0, direction, direction)

    def pair_product(j):
        x = xbuf[2 * j - 1 : 2 * j + 1].reshape(2 * ROWS, FEAT)
        pairs[j - 1] = dot32(x, wg[...])

    for tick in range(QUARTERED + 4):
        if tick < QUARTERED:
            over_z[tick].wait_recv()
            chunk_from(tick, t, 0).start()
            chunk_from(tick, t, 1).start()
        if tick == 0:
            own[...] = dot32(hloc[:, feats(u)], wg[...])
        i = tick - 2
        if 0 <= i < QUARTERED:
            chunk_from(i, t_left, 0).wait_recv()
            chunk_from(i, t_right, 1).wait_recv()
            pass_on(i).start()
        i = tick - 4
        if 0 <= i < QUARTERED:
            remote(
                xbuf.at[i, part(across)], xbuf.at[i, part(across)], fs.at[i], fr.at[i],
                {"tp": t_right},
            ).wait_recv()
            if i == 0:
                far_product()
            elif i % 2 == 0:
                pair_product(i // 2)
            if i == 2:
                for direction in range(2):
                    send_kv(1, direction, 1 - direction)
                    send_kv(1, direction, direction)
                for direction in range(2):
                    send_q(0, direction, direction)
                for direction in range(2):
                    send_q(1, direction, 1 - direction)
    for direction in range(2):
        for piece in range(2):
            send_kv(2, direction, piece)
    over_z[QUARTERED].wait_recv()
    over_z[QUARTERED + 1].wait_recv()
    pair_product(3)
    for direction in range(2):
        for piece in range(2):
            send_kv(3, direction, piece)
    for direction in range(2):
        send_q(1, direction, direction)

    def rotated(x):
        return x * rope[0] + pltpu.roll(x, HEAD // 2, 1) * rope[1]

    for piece in range(2):
        kv_copy(3, 0, piece).wait_recv()
        kv_copy(3, 1, piece).wait_recv()
        x = own[:, PIECE_COLS[piece]]
        x = x + kv_inbox[0, 3, piece].astype(F32)
        x = (x + kv_inbox[1, 3, piece].astype(F32)) * row_scale[...]
        if piece == 0:
            x = rotated(x)
        kv[:, piece * HEAD : (piece + 1) * HEAD] = x.astype(BF16)

    def z_of(i):
        return lax.rem(u + Z_STEPS[i] + NZ, NZ)

    def shard(owner, i):
        return kv_all.at[owner * NZ + z_of(i)]

    def held(i):
        return kv if i == 0 else shard(b, i)

    def z_copy(i, src, dst):
        to = u_right if Z_STEPS[i] < 0 else u_left
        return remote(src, dst, gzs.at[i], gzr.at[i], {"uly": to})

    def x_send(i, direction):
        return remote(
            held(i), shard(b, i), gxs.at[i, direction], gxr.at[i, direction],
            {"blk": b_right if direction == 0 else b_left},
        )

    def x_wait(i, direction):
        source = b_left if direction == 0 else b_right
        return remote(
            shard(source, i), shard(source, i), gxs.at[i, direction], gxr.at[i, direction],
            {"blk": b_right},
        )

    def x_pass(i):
        source, target = (b_left, b_right) if i % 2 == 0 else (b_right, b_left)
        return remote(shard(source, i), shard(source, i), gfs.at[i], gfr.at[i], {"blk": target})

    def side(i, m):
        owner = (b, b_left, b_right, b_across)[m]
        src = held(i) if m == 0 else shard(owner, i)
        return remote(src, shard(owner, i), gss.at[i, m], gsr.at[i, m], {"blk": sibling})

    def side_wait(i, m):
        owner = lax.rem(sibling + (0, 6, 2, 4)[m], 8)
        return remote(shard(owner, i), shard(owner, i), gss.at[i, m], gsr.at[i, m], {"blk": sibling})

    z_sends = []

    def start_z(step, src_i):
        copy = z_copy(Z_STEPS.index(step), held(src_i), shard(b, src_i))
        copy.start()
        z_sends.append(copy)

    place_own = pltpu.make_async_copy(kv, kv_all.at[b * NZ + u], lsem.at[2])

    def gather_tick(tick):
        i = tick
        if i < NZ:
            step = Z_STEPS[i]
            if i == 0:
                start_z(-1, 0)
                start_z(1, 0)
                place_own.start()
            else:
                z_copy(i, shard(b, i), shard(b, i)).wait_recv()
                if -4 < step < 0:
                    start_z(step - 1, i)
                if 0 < step < 3:
                    start_z(step + 1, i)
            x_send(i, 0).start()
            x_send(i, 1).start()
            side(i, 0).start()
        i = tick - 2
        if 0 <= i < NZ:
            x_wait(i, 0).wait_recv()
            x_wait(i, 1).wait_recv()
            x_pass(i).start()
            side(i, 1).start()
            side(i, 2).start()
        i = tick - 4
        if 0 <= i < NZ:
            remote(
                shard(b_across, i), shard(b_across, i), gfs.at[i], gfr.at[i], {"blk": b_right}
            ).wait_recv()
            side(i, 3).start()

    def finish_q(piece):
        q_copy(3, 0, piece).wait_recv()
        q_copy(3, 1, piece).wait_recv()
        cols = PIECE_COLS[2 + piece]
        x = own[:, cols] + q_inbox[0, 3, piece].astype(F32)
        own[:, cols] = (x + q_inbox[1, 3, piece].astype(F32)) * (row_scale[:, :1] * QSCALE)
        for h in range(piece * HEADS // 2, (piece + 1) * HEADS // 2):
            x = rotated(own[:, h * HEAD : (h + 1) * HEAD])
            q_out[h * ROWS : (h + 1) * ROWS, :] = x.astype(BF16)

    gather_tick(0)
    for direction in range(2):
        send_q(2, direction, 1 - direction)
    gather_tick(1)
    gather_tick(2)
    for direction in range(2):
        send_q(2, direction, direction)
    gather_tick(3)
    gather_tick(4)
    for direction in range(2):
        send_q(3, direction, 1 - direction)
    gather_tick(5)
    gather_tick(6)
    for direction in range(2):
        send_q(3, direction, direction)
    gather_tick(7)
    gather_tick(8)
    finish_q(0)
    gather_tick(9)
    finish_q(1)
    gather_tick(10)
    gather_tick(11)
    place_own.wait()
    for i in range(NZ):
        for m in range(4):
            side_wait(i, m).wait_recv()

    for copy in over_z:
        copy.wait_send()
    for i in range(QUARTERED):
        chunk_from(i, t, 0).wait_send()
        chunk_from(i, t, 1).wait_send()
        pass_on(i).wait_send()
    for direction in range(2):
        for step in range(4):
            for piece in range(2):
                if step > 0 or piece == direction:
                    kv_copy(step, direction, piece).wait_send()
                    q_copy(step, direction, piece).wait_send()
    for copy in z_sends:
        copy.wait_send()
    for i in range(NZ):
        x_send(i, 0).wait_send()
        x_send(i, 1).wait_send()
        x_pass(i).wait_send()
        for m in range(4):
            side(i, m).wait_send()


ANY = pl.BlockSpec(memory_space=pl.ANY)
VM = pl.BlockSpec(memory_space=pltpu.VMEM)
DMA = pltpu.SemaphoreType.DMA


HBM = pl.BlockSpec(memory_space=pltpu.HBM)
SM = pl.BlockSpec(memory_space=pltpu.SMEM)


def project(order, freq, gain, hidden, weights):
    n = NZ - 1
    return pl.pallas_call(
        proj_kernel,
        out_shape=(
            jax.ShapeDtypeStruct((HEADS * ROWS, HEAD), BF16),
            jax.ShapeDtypeStruct((8 * NZ, ROWS, 2 * HEAD), BF16),
        ),
        in_specs=[SM, VM, VM, HBM, HBM],
        out_specs=(VM, VM),
        scratch_shapes=[
            pltpu.VMEM((ROWS, NZ * FEAT), BF16),
            pltpu.VMEM((FEAT, COLS), BF16),
            pltpu.VMEM((FEAT, COLS), BF16),
            pltpu.VMEM((NZ * FEAT // 128, 128), F32),
            pltpu.VMEM((n, ROWS, FEAT), BF16),
            pltpu.VMEM((ROWS, COLS), F32),
            pltpu.VMEM((ROWS, COLS), F32),
            pltpu.VMEM((3, 2 * ROWS, COLS), F32),
            pltpu.VMEM((ROWS, 2 * HEAD), BF16),
            pltpu.VMEM((2, ROWS, HEAD), F32),
            pltpu.VMEM((ROWS, HEAD), F32),
            pltpu.VMEM((2, 4, 2, ROWS, HEAD), BF16),
            pltpu.VMEM((2, 4, 2, ROWS, HEAD), BF16),
            pltpu.VMEM((2, 4, 2, ROWS, KCOL // 2), BF16),
            pltpu.VMEM((2, 4, 2, ROWS, KCOL // 2), BF16),
            DMA((3,)),
            DMA((n,)), DMA((n,)),
            DMA((n, 2)), DMA((n, 2)),
            DMA((n,)), DMA((n,)),
            DMA((2, 4, 2)), DMA((2, 4, 2)),
            DMA((2, 4, 2)), DMA((2, 4, 2)),
            DMA((NZ,)), DMA((NZ,)),
            DMA((NZ, 2)), DMA((NZ, 2)),
            DMA((NZ,)), DMA((NZ,)),
            DMA((NZ, 4)), DMA((NZ, 4)),
        ],
        compiler_params=pltpu.CompilerParams(
            collective_id=0, has_side_effects=True, vmem_limit_bytes=62 << 20
        ),
        name="project",
    )(order, freq, gain, hidden, weights)


def attend_kernel(order, docs, q, kv, out, inverse, m_ref, l_ref, acc):
    per = BLOCK // ROWS
    shard = lax.axis_index("blk") * NZ + lax.axis_index("uly")
    q_block = order[shard // per] * per + lax.rem(shard, per)
    for r in range(16):
        inverse[order[r]] = r
    segment = docs[pl.ds(q_block, 1), :]
    starts = jnp.zeros((1, ROWS), jnp.int32)
    for n in range(1, 16):
        before = jnp.sum((docs[...] < n).astype(jnp.int32))
        starts = jnp.where(segment == n, before, starts)
    count = q_block - jnp.min(starts) // ROWS + 1
    wide = HEADS * ROWS
    m_ref[...] = jnp.full((1, wide), NEG_BIG, F32)
    l_ref[...] = jnp.zeros((1, wide), F32)
    acc[...] = jnp.zeros((HEAD, wide), F32)
    lane = lax.broadcasted_iota(jnp.int32, (128, ROWS), 1)
    row = lax.broadcasted_iota(jnp.int32, (128, ROWS), 0)
    causal = row <= lane
    starts = jnp.broadcast_to(starts, (128, ROWS))

    def step(i, carry):
        k_block = q_block - i
        at = inverse[k_block // per] * per + lax.rem(k_block, per)
        k = kv[at, :, :HEAD]
        v = kv[at, :, HEAD:]
        scores = lax.dot_general(
            k, q[...], (((1,), (1,)), ((), ())), preferred_element_type=F32
        )
        allowed = (row + k_block * 128 >= starts) & (causal | (i > 0))
        bias = jnp.where(allowed, 0.0, NEG_BIG)
        scores = scores + jnp.concatenate([bias] * HEADS, axis=1)
        m_old = m_ref[...]
        m_new = jnp.maximum(m_old, jnp.max(scores, axis=0, keepdims=True))
        weights = jnp.exp2(scores - m_new)
        factor = jnp.exp2(m_old - m_new)
        m_ref[...] = m_new
        l_ref[...] = l_ref[...] * factor + jnp.sum(weights, axis=0, keepdims=True)
        mixed = lax.dot_general(
            v, weights.astype(BF16), (((0,), (0,)), ((), ())), preferred_element_type=F32
        )
        acc[...] = acc[...] * factor + mixed
        return carry

    lax.fori_loop(0, count, step, 0)
    result = acc[...] / l_ref[...]
    for h in range(HEADS):
        part = result[:, h * ROWS : (h + 1) * ROWS]
        out[:, h * HEAD : (h + 1) * HEAD] = part.T.astype(BF16)


def attend(order, docs, q, kv):
    wide = HEADS * ROWS
    return pl.pallas_call(
        attend_kernel,
        out_shape=jax.ShapeDtypeStruct((ROWS, HEADS * HEAD), BF16),
        in_specs=[SM, VM, VM, VM],
        out_specs=VM,
        scratch_shapes=[
            pltpu.SMEM((16,), jnp.int32),
            pltpu.VMEM((1, wide), F32),
            pltpu.VMEM((1, wide), F32),
            pltpu.VMEM((HEAD, wide), F32),
        ],
        compiler_params=pltpu.CompilerParams(vmem_limit_bytes=60 << 20),
        name="attend",
    )(order, docs, q, kv)


PIECES = 4
HOPS = 4
PROWS = ROWS // PIECES
OUTW = 1024


def out_kernel(att, w, out, wloc, abuf, far_stage, near_stage, far_box, near_box,
               lsem, zs, zr, fs, fr, ns, nr):
    u = lax.axis_index("uly")
    t = lax.axis_index("tp")
    t_right, t_left = lax.rem(t + 1, NT), lax.rem(t + NT - 1, NT)
    u_right, u_left = lax.rem(u + 1, NZ), lax.rem(u + NZ - 1, NZ)
    load_w = pltpu.make_async_copy(w, wloc, lsem.at[0])
    load_w.start()
    own_copies = []
    for p in range(PIECES):
        copy = pltpu.make_async_copy(att.at[p], abuf.at[u, p], lsem.at[1 + p])
        copy.start()
        own_copies.append(copy)
    greet([{"uly": u_right}, {"uly": u_left}, {"tp": t_right}, {"tp": t_left}])

    def z_hops(p, direction):
        return 4 if (p + direction) % 2 == 0 else 3

    def chunk(direction, h):
        return lax.rem(u + NZ + (-h if direction == 0 else h), NZ)

    def z_copy(p, direction, h, source):
        src = att.at[p] if h == 0 else abuf.at[source, p]
        return remote(
            src, abuf.at[source, p], zs.at[p, direction, h], zr.at[p, direction, h],
            {"uly": u_right if direction == 0 else u_left},
        )

    def z_send(p, direction, h):
        return z_copy(p, direction, h, chunk(direction, h))

    def z_wait(p, direction, h):
        source = chunk(direction, h + 1)
        return remote(
            abuf.at[source, p], abuf.at[source, p], zs.at[p, direction, h],
            zr.at[p, direction, h], {"uly": u_right},
        )

    def z_step(p, h):
        for direction in range(2):
            hops = z_hops(p, direction)
            if h > 0 and h <= hops:
                z_wait(p, direction, h - 1).wait_recv()
            if h < hops:
                z_send(p, direction, h).start()

    def product(p, rel):
        d = lax.rem(t + rel, NT)
        x = abuf[pl.ds(2 * d, 2), p].reshape(2 * PROWS, FEAT)
        return dot32(x, wloc[...])

    def half(side):
        return slice(side * (OUTW // 2), (side + 1) * (OUTW // 2))

    def far_send(p, side):
        return remote(
            far_stage.at[p, side], far_box.at[p, side], fs.at[p, side], fr.at[p, side],
            {"tp": t_right if side == 0 else t_left},
        )

    def near_send(p, direction, side):
        return remote(
            near_stage.at[p, direction, side], near_box.at[p, direction, side],
            ns.at[p, direction, side], nr.at[p, direction, side],
            {"tp": t_right if direction == 0 else t_left},
        )

    def finish(p):
        mine = sides[p]
        for side in range(2):
            near_send(p, 0, side).wait_recv()
            near_send(p, 1, side).wait_recv()
            summed = mine[:, half(side)] + near_box[p, 0, side].astype(F32)
            summed = summed + near_box[p, 1, side].astype(F32)
            out[:, p, :, half(side)] = summed.reshape(2, PROWS, OUTW // 2).astype(BF16)

    z_step(0, 0)
    load_w.wait()
    for copy in own_copies:
        copy.wait()
    sides = {}
    for slot in range(1, PIECES + HOPS + 2):
        for p in range(PIECES):
            if 0 <= slot - p <= HOPS:
                z_step(p, slot - p)
        p = slot - HOPS
        if 0 <= p < PIECES:
            value = product(p, 2)
            for side in range(2):
                far_stage[p, side] = value[:, half(side)].astype(BF16)
                far_send(p, side).start()
            right = product(p, 1)
            near_stage[p, 0, 1] = right[:, half(1)].astype(BF16)
            near_send(p, 0, 1).start()
            left = product(p, 3)
            near_stage[p, 1, 0] = left[:, half(0)].astype(BF16)
            near_send(p, 1, 0).start()
            sides[p] = right[:, half(0)], left[:, half(1)]
        p = slot - HOPS - 1
        if 0 <= p < PIECES:
            right, left = sides[p]
            far_send(p, 0).wait_recv()
            near_stage[p, 0, 0] = (right + far_box[p, 0].astype(F32)).astype(BF16)
            near_send(p, 0, 0).start()
            far_send(p, 1).wait_recv()
            near_stage[p, 1, 1] = (left + far_box[p, 1].astype(F32)).astype(BF16)
            near_send(p, 1, 1).start()
            mine = product(p, 0)
            sides[p] = mine
        p = slot - HOPS - 2
        if 0 <= p < PIECES:
            finish(p)
    for p in range(PIECES):
        for direction in range(2):
            for h in range(z_hops(p, direction)):
                z_send(p, direction, h).wait_send()
            far_send(p, direction).wait_send()
            for side in range(2):
                near_send(p, direction, side).wait_send()


def project_out(attended, w):
    half = OUTW // 2
    out = pl.pallas_call(
        out_kernel,
        out_shape=jax.ShapeDtypeStruct((2, PIECES, PROWS, OUTW), BF16),
        in_specs=[ANY, HBM],
        out_specs=VM,
        scratch_shapes=[
            pltpu.VMEM((FEAT, OUTW), BF16),
            pltpu.VMEM((NZ, PIECES, PROWS, FEAT), BF16),
            pltpu.VMEM((PIECES, 2, 2 * PROWS, half), BF16),
            pltpu.VMEM((PIECES, 2, 2, 2 * PROWS, half), BF16),
            pltpu.VMEM((PIECES, 2, 2 * PROWS, half), BF16),
            pltpu.VMEM((PIECES, 2, 2, 2 * PROWS, half), BF16),
            DMA((1 + PIECES,)),
            DMA((PIECES, 2, 4)), DMA((PIECES, 2, 4)),
            DMA((PIECES, 2)), DMA((PIECES, 2)),
            DMA((PIECES, 2, 2)), DMA((PIECES, 2, 2)),
        ],
        compiler_params=pltpu.CompilerParams(
            collective_id=2, has_side_effects=True, vmem_limit_bytes=62 << 20
        ),
        name="project_out",
    )(attended.reshape(PIECES, PROWS, FEAT), w)
    return out.reshape(2 * ROWS, OUTW)


def rope_frequencies():
    base = THETA ** (-2.0 * np.arange(HEAD // 2, dtype=np.float64) / HEAD)
    wavelen = 2.0 * np.pi / base
    smooth = (8192.0 / wavelen - 1.0) / 3.0
    blended = (1.0 - smooth) * base / 8.0 + smooth * base
    scaled = np.where(wavelen > 8192.0, base / 8.0, np.where(wavelen < 2048.0, base, blended))
    return jnp.asarray(np.tile(scaled, 2)[None, :], F32)


def on_device(hidden, norm_gain, query_key_value_weight, w_out, doc_ids, block_order):
    weights = query_key_value_weight.reshape(FEAT, COLS)
    gain = norm_gain.reshape(NZ * FEAT // 128, 128)
    docs = doc_ids.reshape(NZ * FEAT // 128, 128)
    q, kv_all = project(block_order, rope_frequencies(), gain, hidden, weights)
    attended = attend(block_order, docs, q, kv_all)
    return project_out(attended, w_out)


def solution(mesh):
    return jax.shard_map(
        on_device,
        mesh=mesh,
        in_specs=(P(("blk", "uly"), None), P(), P("uly", "tp", None), P("tp", "uly"), P(), P()),
        out_specs=P(("blk", "tp"), "uly"),
        check_vma=False,
    )
```

```python
import math

import jax
import jax.numpy as jnp
import numpy as np
from jax import lax
from jax.experimental import pallas as pl
from jax.experimental.pallas import tpu as pltpu
from jax.sharding import PartitionSpec as P

HEAD = 128
HEADS = 8
BLOCK = 512
THETA = 500000.0
NEG_BIG = -1e30
NZ = 8
NT = 4
ROWS = 128
SUB = ROWS // NT
FEAT = 1024
COLS = (HEADS + 2) * HEAD
MESH = pl.DeviceIdType.MESH
F32 = jnp.float32
BF16 = jnp.bfloat16
FAR_FIRST = (4, 3, 5, 2, 6, 1, 7)
QSCALE = math.log2(math.e) / math.sqrt(HEAD)


def remote(src, dst, send_sem, recv_sem, device):
    return pltpu.make_async_remote_copy(
        src_ref=src,
        dst_ref=dst,
        send_sem=send_sem,
        recv_sem=recv_sem,
        device_id=device,
        device_id_type=MESH,
    )


def greet(devices):
    barrier = pltpu.get_barrier_semaphore()
    for device in devices:
        pl.semaphore_signal(barrier, inc=1, device_id=device, device_id_type=MESH)
    pl.semaphore_wait(barrier, len(devices))


def dot32(a, b):
    return jnp.dot(a, b, preferred_element_type=F32)


KCOL = HEADS * HEAD
PIECE_COLS = (slice(KCOL, KCOL + HEAD), slice(KCOL + HEAD, COLS), slice(0, KCOL // 2), slice(KCOL // 2, KCOL))
QUARTERED = 5
Z_STEPS = (0, -1, 1, -2, 2, -3, 3, -4)


def proj_kernel(
    order, freq, gain, hid, w, q_out, kv_all,
    hloc, wloc, wg, g32, xbuf, own, far, pairs, kv, rope, row_scale,
    kv_stage, kv_inbox, q_stage, q_inbox,
    lsem, zs, zr, ys, yr, fs, fr, ks, kr, qs, qr,
    gzs, gzr, gxs, gxr, gfs, gfr, gss, gsr,
):
    b = lax.axis_index("blk")
    u = lax.axis_index("uly")
    t = lax.axis_index("tp")
    t_right, t_left, across = lax.rem(t + 1, NT), lax.rem(t + 3, NT), lax.rem(t + 2, NT)
    u_right, u_left = lax.rem(u + 1, NZ), lax.rem(u + NZ - 1, NZ)
    b_right, b_left, b_across = lax.rem(b + 2, 8), lax.rem(b + 6, 8), lax.rem(b + 4, 8)
    sibling = b + 1 - 2 * lax.rem(b, 2)
    load_w = pltpu.make_async_copy(w, wloc, lsem.at[0])
    load_h = pltpu.make_async_copy(hid, hloc, lsem.at[1])
    load_w.start()
    load_h.start()
    greet(
        [{"uly": lax.rem(u + k, NZ)} for k in range(1, NZ)]
        + [{"tp": t_right}, {"tp": t_left}, {"blk": b_right}, {"blk": b_left}, {"blk": sibling}]
    )

    def part(owner):
        return pl.ds(pl.multiple_of(owner * SUB, SUB), SUB)

    def feats(owner):
        return pl.ds(pl.multiple_of(owner * FEAT, FEAT), FEAT)

    over_z = []
    for i, k in enumerate(FAR_FIRST):
        v = lax.rem(u + NZ - k, NZ)
        if i < QUARTERED:
            src, dst = hid.at[part(t), feats(v)], xbuf.at[i, part(t)]
        else:
            src, dst = hid.at[:, feats(v)], xbuf.at[i]
        copy = remote(src, dst, zs.at[i], zr.at[i], {"uly": v})
        copy.start()
        over_z.append(copy)

    g32[...] = gain[...].astype(F32)
    load_w.wait()

    def fold(c, carry):
        r = pl.ds(pl.multiple_of(c * 128, 128), 128)
        column = jnp.broadcast_to(g32[pl.ds(u * NZ + c, 1), :], (128, 128)).T
        for n in range(COLS // 128):
            lanes = slice(n * 128, (n + 1) * 128)
            wg[r, lanes] = (wloc[r, lanes].astype(F32) * column).astype(BF16)
        return carry

    lax.fori_loop(0, FEAT // 128, fold, 0)
    load_h.wait()

    def square(c, acc):
        x = hloc[:, pl.ds(pl.multiple_of(c * 128, 128), 128)].astype(F32)
        return acc + x * x

    total = lax.fori_loop(0, NZ * FEAT // 128, square, jnp.zeros((ROWS, 128), F32))
    mean = jnp.sum(total, axis=1, keepdims=True) / (NZ * FEAT)
    row_scale[...] = jnp.broadcast_to(lax.rsqrt(mean + 1e-05), (ROWS, HEAD))
    shard_id = b * NZ + u
    block = shard_id // (BLOCK // ROWS)
    first = order[block] * BLOCK + lax.rem(shard_id, BLOCK // ROWS) * ROWS
    position = (lax.broadcasted_iota(jnp.int32, (ROWS, HEAD), 0) + first).astype(F32)
    angles = position * freq[...]
    left_half = lax.broadcasted_iota(jnp.int32, (ROWS, HEAD), 1) < HEAD // 2
    sines = jnp.sin(angles)
    rope[0] = jnp.cos(angles)
    rope[1] = jnp.where(left_half, -sines, sines)

    def chunk_from(i, source, direction):
        return remote(
            xbuf.at[i, part(source)], xbuf.at[i, part(source)],
            ys.at[i, direction], yr.at[i, direction],
            {"tp": t_right if direction == 0 else t_left},
        )

    def pass_on(i):
        source, target = (t_left, t_right) if i % 2 == 0 else (t_right, t_left)
        return remote(
            xbuf.at[i, part(source)], xbuf.at[i, part(source)], fs.at[i], fr.at[i], {"tp": target}
        )

    def kv_copy(step, direction, piece):
        return remote(
            kv_stage.at[direction, step, piece], kv_inbox.at[direction, step, piece],
            ks.at[direction, step, piece], kr.at[direction, step, piece],
            {"uly": u_right if direction == 0 else u_left},
        )

    def q_copy(step, direction, piece):
        return remote(
            q_stage.at[direction, step, piece], q_inbox.at[direction, step, piece],
            qs.at[direction, step, piece], qr.at[direction, step, piece],
            {"uly": u_right if direction == 0 else u_left},
        )

    def mine(step, direction, cols):
        if step == 0:
            return far[:, cols]
        return pairs[step - 1, direction * ROWS : (direction + 1) * ROWS, cols]

    def send_kv(step, direction, piece):
        value = mine(step, direction, PIECE_COLS[piece])
        if step > 1 or (step == 1 and piece == direction):
            kv_copy(step - 1, direction, piece).wait_recv()
            value = value + kv_inbox[direction, step - 1, piece].astype(F32)
        kv_stage[direction, step, piece] = value.astype(BF16)
        kv_copy(step, direction, piece).start()

    def send_q(step, direction, piece):
        value = mine(step, direction, PIECE_COLS[2 + piece])
        if step > 1 or (step == 1 and piece == direction):
            q_copy(step - 1, direction, piece).wait_recv()
            value = value + q_inbox[direction, step - 1, piece].astype(F32)
        q_stage[direction, step, piece] = value.astype(BF16)
        q_copy(step, direction, piece).start()

    def far_product():
        far[...] = dot32(xbuf[0], wg[...])
        for direction in range(2):
            send_kv(0, direction, direction)

    def pair_product(j):
        x = xbuf[2 * j - 1 : 2 * j + 1].reshape(2 * ROWS, FEAT)
        pairs[j - 1] = dot32(x, wg[...])

    for tick in range(QUARTERED + 4):
        if tick < QUARTERED:
            over_z[tick].wait_recv()
            chunk_from(tick, t, 0).start()
            chunk_from(tick, t, 1).start()
        if tick == 0:
            own[...] = dot32(hloc[:, feats(u)], wg[...])
        i = tick - 2
        if 0 <= i < QUARTERED:
            chunk_from(i, t_left, 0).wait_recv()
            chunk_from(i, t_right, 1).wait_recv()
            pass_on(i).start()
        i = tick - 4
        if 0 <= i < QUARTERED:
            remote(
                xbuf.at[i, part(across)], xbuf.at[i, part(across)], fs.at[i], fr.at[i],
                {"tp": t_right},
            ).wait_recv()
            if i == 0:
                far_product()
            elif i % 2 == 0:
                pair_product(i // 2)
            if i == 2:
                for direction in range(2):
                    send_kv(1, direction, 1 - direction)
                    send_kv(1, direction, direction)
                for direction in range(2):
                    send_q(0, direction, direction)
                for direction in range(2):
                    send_q(1, direction, 1 - direction)
    for direction in range(2):
        for piece in range(2):
            send_kv(2, direction, piece)
    over_z[QUARTERED].wait_recv()
    over_z[QUARTERED + 1].wait_recv()
    pair_product(3)
    for direction in range(2):
        for piece in range(2):
            send_kv(3, direction, piece)
    for direction in range(2):
        send_q(1, direction, direction)

    def rotated(x):
        return x * rope[0] + pltpu.roll(x, HEAD // 2, 1) * rope[1]

    for piece in range(2):
        kv_copy(3, 0, piece).wait_recv()
        kv_copy(3, 1, piece).wait_recv()
        x = own[:, PIECE_COLS[piece]]
        x = x + kv_inbox[0, 3, piece].astype(F32)
        x = (x + kv_inbox[1, 3, piece].astype(F32)) * row_scale[...]
        if piece == 0:
            x = rotated(x)
        kv[:, piece * HEAD : (piece + 1) * HEAD] = x.astype(BF16)

    def z_of(i):
        return lax.rem(u + Z_STEPS[i] + NZ, NZ)

    def shard(owner, i):
        return kv_all.at[owner * NZ + z_of(i)]

    def held(i):
        return kv if i == 0 else shard(b, i)

    def z_copy(i, src, dst):
        to = u_right if Z_STEPS[i] < 0 else u_left
        return remote(src, dst, gzs.at[i], gzr.at[i], {"uly": to})

    def x_send(i, direction):
        return remote(
            held(i), shard(b, i), gxs.at[i, direction], gxr.at[i, direction],
            {"blk": b_right if direction == 0 else b_left},
        )

    def x_wait(i, direction):
        source = b_left if direction == 0 else b_right
        return remote(
            shard(source, i), shard(source, i), gxs.at[i, direction], gxr.at[i, direction],
            {"blk": b_right},
        )

    def x_pass(i):
        source, target = (b_left, b_right) if i % 2 == 0 else (b_right, b_left)
        return remote(shard(source, i), shard(source, i), gfs.at[i], gfr.at[i], {"blk": target})

    def side(i, m):
        owner = (b, b_left, b_right, b_across)[m]
        src = held(i) if m == 0 else shard(owner, i)
        return remote(src, shard(owner, i), gss.at[i, m], gsr.at[i, m], {"blk": sibling})

    def side_wait(i, m):
        owner = lax.rem(sibling + (0, 6, 2, 4)[m], 8)
        return remote(shard(owner, i), shard(owner, i), gss.at[i, m], gsr.at[i, m], {"blk": sibling})

    z_sends = []

    def start_z(step, src_i):
        copy = z_copy(Z_STEPS.index(step), held(src_i), shard(b, src_i))
        copy.start()
        z_sends.append(copy)

    place_own = pltpu.make_async_copy(kv, kv_all.at[b * NZ + u], lsem.at[2])

    def gather_tick(tick):
        i = tick
        if i < NZ:
            step = Z_STEPS[i]
            if i == 0:
                start_z(-1, 0)
                start_z(1, 0)
                place_own.start()
            else:
                z_copy(i, shard(b, i), shard(b, i)).wait_recv()
                if -4 < step < 0:
                    start_z(step - 1, i)
                if 0 < step < 3:
                    start_z(step + 1, i)
            x_send(i, 0).start()
            x_send(i, 1).start()
            side(i, 0).start()
        i = tick - 2
        if 0 <= i < NZ:
            x_wait(i, 0).wait_recv()
            x_wait(i, 1).wait_recv()
            x_pass(i).start()
            side(i, 1).start()
            side(i, 2).start()
        i = tick - 4
        if 0 <= i < NZ:
            remote(
                shard(b_across, i), shard(b_across, i), gfs.at[i], gfr.at[i], {"blk": b_right}
            ).wait_recv()
            side(i, 3).start()

    def finish_q(piece):
        q_copy(3, 0, piece).wait_recv()
        q_copy(3, 1, piece).wait_recv()
        cols = PIECE_COLS[2 + piece]
        x = own[:, cols] + q_inbox[0, 3, piece].astype(F32)
        own[:, cols] = (x + q_inbox[1, 3, piece].astype(F32)) * (row_scale[:, :1] * QSCALE)
        for h in range(piece * HEADS // 2, (piece + 1) * HEADS // 2):
            x = rotated(own[:, h * HEAD : (h + 1) * HEAD])
            q_out[h * ROWS : (h + 1) * ROWS, :] = x.astype(BF16)

    gather_tick(0)
    for direction in range(2):
        send_q(2, direction, 1 - direction)
    gather_tick(1)
    gather_tick(2)
    for direction in range(2):
        send_q(2, direction, direction)
    gather_tick(3)
    gather_tick(4)
    for direction in range(2):
        send_q(3, direction, 1 - direction)
    gather_tick(5)
    gather_tick(6)
    for direction in range(2):
        send_q(3, direction, direction)
    gather_tick(7)
    gather_tick(8)
    finish_q(0)
    gather_tick(9)
    finish_q(1)
    gather_tick(10)
    gather_tick(11)
    place_own.wait()
    for i in range(NZ):
        for m in range(4):
            side_wait(i, m).wait_recv()

    for copy in over_z:
        copy.wait_send()
    for i in range(QUARTERED):
        chunk_from(i, t, 0).wait_send()
        chunk_from(i, t, 1).wait_send()
        pass_on(i).wait_send()
    for direction in range(2):
        for step in range(4):
            for piece in range(2):
                if step > 0 or piece == direction:
                    kv_copy(step, direction, piece).wait_send()
                    q_copy(step, direction, piece).wait_send()
    for copy in z_sends:
        copy.wait_send()
    for i in range(NZ):
        x_send(i, 0).wait_send()
        x_send(i, 1).wait_send()
        x_pass(i).wait_send()
        for m in range(4):
            side(i, m).wait_send()


ANY = pl.BlockSpec(memory_space=pl.ANY)
VM = pl.BlockSpec(memory_space=pltpu.VMEM)
DMA = pltpu.SemaphoreType.DMA


HBM = pl.BlockSpec(memory_space=pltpu.HBM)
SM = pl.BlockSpec(memory_space=pltpu.SMEM)


def project(order, freq, gain, hidden, weights):
    n = NZ - 1
    return pl.pallas_call(
        proj_kernel,
        out_shape=(
            jax.ShapeDtypeStruct((HEADS * ROWS, HEAD), BF16),
            jax.ShapeDtypeStruct((8 * NZ, ROWS, 2 * HEAD), BF16),
        ),
        in_specs=[SM, VM, VM, HBM, HBM],
        out_specs=(VM, VM),
        scratch_shapes=[
            pltpu.VMEM((ROWS, NZ * FEAT), BF16),
            pltpu.VMEM((FEAT, COLS), BF16),
            pltpu.VMEM((FEAT, COLS), BF16),
            pltpu.VMEM((NZ * FEAT // 128, 128), F32),
            pltpu.VMEM((n, ROWS, FEAT), BF16),
            pltpu.VMEM((ROWS, COLS), F32),
            pltpu.VMEM((ROWS, COLS), F32),
            pltpu.VMEM((3, 2 * ROWS, COLS), F32),
            pltpu.VMEM((ROWS, 2 * HEAD), BF16),
            pltpu.VMEM((2, ROWS, HEAD), F32),
            pltpu.VMEM((ROWS, HEAD), F32),
            pltpu.VMEM((2, 4, 2, ROWS, HEAD), BF16),
            pltpu.VMEM((2, 4, 2, ROWS, HEAD), BF16),
            pltpu.VMEM((2, 4, 2, ROWS, KCOL // 2), BF16),
            pltpu.VMEM((2, 4, 2, ROWS, KCOL // 2), BF16),
            DMA((3,)),
            DMA((n,)), DMA((n,)),
            DMA((n, 2)), DMA((n, 2)),
            DMA((n,)), DMA((n,)),
            DMA((2, 4, 2)), DMA((2, 4, 2)),
            DMA((2, 4, 2)), DMA((2, 4, 2)),
            DMA((NZ,)), DMA((NZ,)),
            DMA((NZ, 2)), DMA((NZ, 2)),
            DMA((NZ,)), DMA((NZ,)),
            DMA((NZ, 4)), DMA((NZ, 4)),
        ],
        compiler_params=pltpu.CompilerParams(
            collective_id=0, has_side_effects=True, vmem_limit_bytes=62 << 20
        ),
        name="project",
    )(order, freq, gain, hidden, weights)


def attend_kernel(order, docs, q, kv, out, inverse, m_ref, l_ref, acc):
    per = BLOCK // ROWS
    shard = lax.axis_index("blk") * NZ + lax.axis_index("uly")
    q_block = order[shard // per] * per + lax.rem(shard, per)
    for r in range(16):
        inverse[order[r]] = r
    segment = docs[pl.ds(q_block, 1), :]
    starts = jnp.zeros((1, ROWS), jnp.int32)
    for n in range(1, 16):
        before = jnp.sum((docs[...] < n).astype(jnp.int32))
        starts = jnp.where(segment == n, before, starts)
    count = q_block - jnp.min(starts) // ROWS + 1
    wide = HEADS * ROWS
    m_ref[...] = jnp.full((1, wide), NEG_BIG, F32)
    l_ref[...] = jnp.zeros((1, wide), F32)
    acc[...] = jnp.zeros((HEAD, wide), F32)
    lane = lax.broadcasted_iota(jnp.int32, (128, ROWS), 1)
    row = lax.broadcasted_iota(jnp.int32, (128, ROWS), 0)
    causal = row <= lane
    starts = jnp.broadcast_to(starts, (128, ROWS))

    def place(k_block):
        k_block = jnp.maximum(k_block, 0)
        return inverse[k_block // per] * per + lax.rem(k_block, per)

    def scores_of(i):
        k_block = q_block - i
        scores = lax.dot_general(
            kv[place(k_block), :, :HEAD], q[...], (((1,), (1,)), ((), ())), preferred_element_type=F32
        )
        allowed = (row + k_block * 128 >= starts) & (causal | (i > 0))
        bias = jnp.where(allowed, 0.0, NEG_BIG)
        return scores + jnp.concatenate([bias] * HEADS, axis=1)

    def mix(i, weights):
        return lax.dot_general(
            kv[place(q_block - i), :, HEAD:], weights.astype(BF16), (((0,), (0,)), ((), ())),
            preferred_element_type=F32,
        )

    def step(j, carry):
        near, past = scores_of(2 * j), scores_of(2 * j + 1)
        m_old = m_ref[...]
        m_new = jnp.maximum(m_old, jnp.max(jnp.maximum(near, past), axis=0, keepdims=True))
        near, past = jnp.exp2(near - m_new), jnp.exp2(past - m_new)
        factor = jnp.exp2(m_old - m_new)
        m_ref[...] = m_new
        l_ref[...] = l_ref[...] * factor + jnp.sum(near + past, axis=0, keepdims=True)
        acc[...] = acc[...] * factor + (mix(2 * j, near) + mix(2 * j + 1, past))
        return carry

    lax.fori_loop(0, (count + 1) // 2, step, 0)
    result = acc[...] / l_ref[...]
    for h in range(HEADS):
        part = result[:, h * ROWS : (h + 1) * ROWS]
        out[:, h * HEAD : (h + 1) * HEAD] = part.T.astype(BF16)


def attend(order, docs, q, kv):
    wide = HEADS * ROWS
    return pl.pallas_call(
        attend_kernel,
        out_shape=jax.ShapeDtypeStruct((ROWS, HEADS * HEAD), BF16),
        in_specs=[SM, VM, VM, VM],
        out_specs=VM,
        scratch_shapes=[
            pltpu.SMEM((16,), jnp.int32),
            pltpu.VMEM((1, wide), F32),
            pltpu.VMEM((1, wide), F32),
            pltpu.VMEM((HEAD, wide), F32),
        ],
        compiler_params=pltpu.CompilerParams(vmem_limit_bytes=60 << 20),
        name="attend",
    )(order, docs, q, kv)


PIECES = 4
HOPS = 4
PROWS = ROWS // PIECES
OUTW = 1024


def out_kernel(att, w, out, wloc, abuf, far_stage, near_stage, far_box, near_box,
               lsem, zs, zr, fs, fr, ns, nr):
    u = lax.axis_index("uly")
    t = lax.axis_index("tp")
    t_right, t_left = lax.rem(t + 1, NT), lax.rem(t + NT - 1, NT)
    u_right, u_left = lax.rem(u + 1, NZ), lax.rem(u + NZ - 1, NZ)
    load_w = pltpu.make_async_copy(w, wloc, lsem.at[0])
    load_w.start()
    own_copies = []
    for p in range(PIECES):
        copy = pltpu.make_async_copy(att.at[p], abuf.at[u, p], lsem.at[1 + p])
        copy.start()
        own_copies.append(copy)
    greet([{"uly": u_right}, {"uly": u_left}, {"tp": t_right}, {"tp": t_left}])

    def z_hops(p, direction):
        return 4 if (p + direction) % 2 == 0 else 3

    def chunk(direction, h):
        return lax.rem(u + NZ + (-h if direction == 0 else h), NZ)

    def z_copy(p, direction, h, source):
        src = att.at[p] if h == 0 else abuf.at[source, p]
        return remote(
            src, abuf.at[source, p], zs.at[p, direction, h], zr.at[p, direction, h],
            {"uly": u_right if direction == 0 else u_left},
        )

    def z_send(p, direction, h):
        return z_copy(p, direction, h, chunk(direction, h))

    def z_wait(p, direction, h):
        source = chunk(direction, h + 1)
        return remote(
            abuf.at[source, p], abuf.at[source, p], zs.at[p, direction, h],
            zr.at[p, direction, h], {"uly": u_right},
        )

    def z_step(p, h):
        for direction in range(2):
            hops = z_hops(p, direction)
            if h > 0 and h <= hops:
                z_wait(p, direction, h - 1).wait_recv()
            if h < hops:
                z_send(p, direction, h).start()

    def product(p, rel):
        d = lax.rem(t + rel, NT)
        x = abuf[pl.ds(2 * d, 2), p].reshape(2 * PROWS, FEAT)
        return dot32(x, wloc[...])

    def half(side):
        return slice(side * (OUTW // 2), (side + 1) * (OUTW // 2))

    def far_send(p, side):
        return remote(
            far_stage.at[p, side], far_box.at[p, side], fs.at[p, side], fr.at[p, side],
            {"tp": t_right if side == 0 else t_left},
        )

    def near_send(p, direction, side):
        return remote(
            near_stage.at[p, direction, side], near_box.at[p, direction, side],
            ns.at[p, direction, side], nr.at[p, direction, side],
            {"tp": t_right if direction == 0 else t_left},
        )

    def finish(p):
        mine = sides[p]
        for side in range(2):
            near_send(p, 0, side).wait_recv()
            near_send(p, 1, side).wait_recv()
            summed = mine[:, half(side)] + near_box[p, 0, side].astype(F32)
            summed = summed + near_box[p, 1, side].astype(F32)
            out[:, p, :, half(side)] = summed.reshape(2, PROWS, OUTW // 2).astype(BF16)

    z_step(0, 0)
    load_w.wait()
    for copy in own_copies:
        copy.wait()
    sides = {}
    for slot in range(1, PIECES + HOPS + 2):
        for p in range(PIECES):
            if 0 <= slot - p <= HOPS:
                z_step(p, slot - p)
        p = slot - HOPS
        if 0 <= p < PIECES:
            value = product(p, 2)
            for side in range(2):
                far_stage[p, side] = value[:, half(side)].astype(BF16)
                far_send(p, side).start()
            right = product(p, 1)
            near_stage[p, 0, 1] = right[:, half(1)].astype(BF16)
            near_send(p, 0, 1).start()
            left = product(p, 3)
            near_stage[p, 1, 0] = left[:, half(0)].astype(BF16)
            near_send(p, 1, 0).start()
            sides[p] = right[:, half(0)], left[:, half(1)]
        p = slot - HOPS - 1
        if 0 <= p < PIECES:
            right, left = sides[p]
            far_send(p, 0).wait_recv()
            near_stage[p, 0, 0] = (right + far_box[p, 0].astype(F32)).astype(BF16)
            near_send(p, 0, 0).start()
            far_send(p, 1).wait_recv()
            near_stage[p, 1, 1] = (left + far_box[p, 1].astype(F32)).astype(BF16)
            near_send(p, 1, 1).start()
            mine = product(p, 0)
            sides[p] = mine
        p = slot - HOPS - 2
        if 0 <= p < PIECES:
            finish(p)
    for p in range(PIECES):
        for direction in range(2):
            for h in range(z_hops(p, direction)):
                z_send(p, direction, h).wait_send()
            far_send(p, direction).wait_send()
            for side in range(2):
                near_send(p, direction, side).wait_send()


def project_out(attended, w):
    half = OUTW // 2
    out = pl.pallas_call(
        out_kernel,
        out_shape=jax.ShapeDtypeStruct((2, PIECES, PROWS, OUTW), BF16),
        in_specs=[ANY, HBM],
        out_specs=VM,
        scratch_shapes=[
            pltpu.VMEM((FEAT, OUTW), BF16),
            pltpu.VMEM((NZ, PIECES, PROWS, FEAT), BF16),
            pltpu.VMEM((PIECES, 2, 2 * PROWS, half), BF16),
            pltpu.VMEM((PIECES, 2, 2, 2 * PROWS, half), BF16),
            pltpu.VMEM((PIECES, 2, 2 * PROWS, half), BF16),
            pltpu.VMEM((PIECES, 2, 2, 2 * PROWS, half), BF16),
            DMA((1 + PIECES,)),
            DMA((PIECES, 2, 4)), DMA((PIECES, 2, 4)),
            DMA((PIECES, 2)), DMA((PIECES, 2)),
            DMA((PIECES, 2, 2)), DMA((PIECES, 2, 2)),
        ],
        compiler_params=pltpu.CompilerParams(
            collective_id=2, has_side_effects=True, vmem_limit_bytes=62 << 20
        ),
        name="project_out",
    )(attended.reshape(PIECES, PROWS, FEAT), w)
    return out.reshape(2 * ROWS, OUTW)


def rope_frequencies():
    base = THETA ** (-2.0 * np.arange(HEAD // 2, dtype=np.float64) / HEAD)
    wavelen = 2.0 * np.pi / base
    smooth = (8192.0 / wavelen - 1.0) / 3.0
    blended = (1.0 - smooth) * base / 8.0 + smooth * base
    scaled = np.where(wavelen > 8192.0, base / 8.0, np.where(wavelen < 2048.0, base, blended))
    return jnp.asarray(np.tile(scaled, 2)[None, :], F32)


def on_device(hidden, norm_gain, query_key_value_weight, w_out, doc_ids, block_order):
    weights = query_key_value_weight.reshape(FEAT, COLS)
    gain = norm_gain.reshape(NZ * FEAT // 128, 128)
    docs = doc_ids.reshape(NZ * FEAT // 128, 128)
    q, kv_all = project(block_order, rope_frequencies(), gain, hidden, weights)
    attended = attend(block_order, docs, q, kv_all)
    return project_out(attended, w_out)


def solution(mesh):
    return jax.shard_map(
        on_device,
        mesh=mesh,
        in_specs=(P(("blk", "uly"), None), P(), P("uly", "tp", None), P("tp", "uly"), P(), P()),
        out_specs=P(("blk", "tp"), "uly"),
        check_vma=False,
    )
```

```python
import math

import jax
import jax.numpy as jnp
import numpy as np
from jax import lax
from jax.experimental import pallas as pl
from jax.experimental.pallas import tpu as pltpu
from jax.sharding import PartitionSpec as P

HEAD = 128
HEADS = 8
BLOCK = 512
THETA = 500000.0
NEG_BIG = -1e30
NZ = 8
NT = 4
ROWS = 128
SUB = ROWS // NT
FEAT = 1024
COLS = (HEADS + 2) * HEAD
MESH = pl.DeviceIdType.MESH
F32 = jnp.float32
BF16 = jnp.bfloat16
FAR_FIRST = (4, 3, 5, 2, 6, 1, 7)
QSCALE = math.log2(math.e) / math.sqrt(HEAD)


def remote(src, dst, send_sem, recv_sem, device):
    return pltpu.make_async_remote_copy(
        src_ref=src,
        dst_ref=dst,
        send_sem=send_sem,
        recv_sem=recv_sem,
        device_id=device,
        device_id_type=MESH,
    )


def greet(devices):
    barrier = pltpu.get_barrier_semaphore()
    for device in devices:
        pl.semaphore_signal(barrier, inc=1, device_id=device, device_id_type=MESH)
    pl.semaphore_wait(barrier, len(devices))


def dot32(a, b):
    return jnp.dot(a, b, preferred_element_type=F32)


KCOL = HEADS * HEAD
PIECE_COLS = (slice(KCOL, KCOL + HEAD), slice(KCOL + HEAD, COLS), slice(0, KCOL // 2), slice(KCOL // 2, KCOL))
QUARTERED = 5
Z_STEPS = (0, -1, 1, -2, 2, -3, 3, -4)


def proj_kernel(
    order, freq, gain, hid, w, q_out, kv_all,
    hloc, wloc, wg, g32, xbuf, own, far, pairs, kv, rope, row_scale,
    kv_stage, kv_inbox, q_stage, q_inbox,
    lsem, zs, zr, ys, yr, fs, fr, ks, kr, qs, qr,
    gzs, gzr, gxs, gxr, gfs, gfr, gss, gsr,
):
    b = lax.axis_index("blk")
    u = lax.axis_index("uly")
    t = lax.axis_index("tp")
    t_right, t_left, across = lax.rem(t + 1, NT), lax.rem(t + 3, NT), lax.rem(t + 2, NT)
    u_right, u_left = lax.rem(u + 1, NZ), lax.rem(u + NZ - 1, NZ)
    b_right, b_left, b_across = lax.rem(b + 2, 8), lax.rem(b + 6, 8), lax.rem(b + 4, 8)
    sibling = b + 1 - 2 * lax.rem(b, 2)
    load_w = pltpu.make_async_copy(w, wloc, lsem.at[0])
    load_h = pltpu.make_async_copy(hid, hloc, lsem.at[1])
    load_w.start()
    load_h.start()
    greet(
        [{"uly": lax.rem(u + k, NZ)} for k in range(1, NZ)]
        + [{"tp": t_right}, {"tp": t_left}, {"blk": b_right}, {"blk": b_left}, {"blk": sibling}]
    )

    def part(owner):
        return pl.ds(pl.multiple_of(owner * SUB, SUB), SUB)

    def feats(owner):
        return pl.ds(pl.multiple_of(owner * FEAT, FEAT), FEAT)

    over_z = []
    for i, k in enumerate(FAR_FIRST):
        v = lax.rem(u + NZ - k, NZ)
        if i < QUARTERED:
            src, dst = hid.at[part(t), feats(v)], xbuf.at[i, part(t)]
        else:
            src, dst = hid.at[:, feats(v)], xbuf.at[i]
        copy = remote(src, dst, zs.at[i], zr.at[i], {"uly": v})
        copy.start()
        over_z.append(copy)

    g32[...] = gain[...].astype(F32)
    load_w.wait()

    def fold(c, carry):
        r = pl.ds(pl.multiple_of(c * 128, 128), 128)
        column = jnp.broadcast_to(g32[pl.ds(u * NZ + c, 1), :], (128, 128)).T
        for n in range(COLS // 128):
            lanes = slice(n * 128, (n + 1) * 128)
            wg[r, lanes] = (wloc[r, lanes].astype(F32) * column).astype(BF16)
        return carry

    lax.fori_loop(0, FEAT // 128, fold, 0)
    load_h.wait()

    def square(c, acc):
        x = hloc[:, pl.ds(pl.multiple_of(c * 128, 128), 128)].astype(F32)
        return acc + x * x

    total = lax.fori_loop(0, NZ * FEAT // 128, square, jnp.zeros((ROWS, 128), F32))
    mean = jnp.sum(total, axis=1, keepdims=True) / (NZ * FEAT)
    row_scale[...] = jnp.broadcast_to(lax.rsqrt(mean + 1e-05), (ROWS, HEAD))
    shard_id = b * NZ + u
    block = shard_id // (BLOCK // ROWS)
    first = order[block] * BLOCK + lax.rem(shard_id, BLOCK // ROWS) * ROWS
    position = (lax.broadcasted_iota(jnp.int32, (ROWS, HEAD), 0) + first).astype(F32)
    angles = position * freq[...]
    left_half = lax.broadcasted_iota(jnp.int32, (ROWS, HEAD), 1) < HEAD // 2
    sines = jnp.sin(angles)
    rope[0] = jnp.cos(angles)
    rope[1] = jnp.where(left_half, -sines, sines)

    def chunk_from(i, source, direction):
        return remote(
            xbuf.at[i, part(source)], xbuf.at[i, part(source)],
            ys.at[i, direction], yr.at[i, direction],
            {"tp": t_right if direction == 0 else t_left},
        )

    def pass_on(i):
        source, target = (t_left, t_right) if i % 2 == 0 else (t_right, t_left)
        return remote(
            xbuf.at[i, part(source)], xbuf.at[i, part(source)], fs.at[i], fr.at[i], {"tp": target}
        )

    def kv_copy(step, direction, piece):
        return remote(
            kv_stage.at[direction, step, piece], kv_inbox.at[direction, step, piece],
            ks.at[direction, step, piece], kr.at[direction, step, piece],
            {"uly": u_right if direction == 0 else u_left},
        )

    def q_copy(step, direction, piece):
        return remote(
            q_stage.at[direction, step, piece], q_inbox.at[direction, step, piece],
            qs.at[direction, step, piece], qr.at[direction, step, piece],
            {"uly": u_right if direction == 0 else u_left},
        )

    def mine(step, direction, cols):
        if step == 0:
            return far[:, cols]
        return pairs[step - 1, direction * ROWS : (direction + 1) * ROWS, cols]

    def send_kv(step, direction, piece):
        value = mine(step, direction, PIECE_COLS[piece])
        if step > 1 or (step == 1 and piece == direction):
            kv_copy(step - 1, direction, piece).wait_recv()
            value = value + kv_inbox[direction, step - 1, piece].astype(F32)
        kv_stage[direction, step, piece] = value.astype(BF16)
        kv_copy(step, direction, piece).start()

    def send_q(step, direction, piece):
        value = mine(step, direction, PIECE_COLS[2 + piece])
        if step > 1 or (step == 1 and piece == direction):
            q_copy(step - 1, direction, piece).wait_recv()
            value = value + q_inbox[direction, step - 1, piece].astype(F32)
        q_stage[direction, step, piece] = value.astype(BF16)
        q_copy(step, direction, piece).start()

    def far_product():
        far[...] = dot32(xbuf[0], wg[...])
        for direction in range(2):
            send_kv(0, direction, direction)

    def pair_product(j):
        x = xbuf[2 * j - 1 : 2 * j + 1].reshape(2 * ROWS, FEAT)
        pairs[j - 1] = dot32(x, wg[...])

    for tick in range(QUARTERED + 4):
        if tick < QUARTERED:
            over_z[tick].wait_recv()
            chunk_from(tick, t, 0).start()
            chunk_from(tick, t, 1).start()
        if tick == 0:
            own[...] = dot32(hloc[:, feats(u)], wg[...])
        i = tick - 2
        if 0 <= i < QUARTERED:
            chunk_from(i, t_left, 0).wait_recv()
            chunk_from(i, t_right, 1).wait_recv()
            pass_on(i).start()
        i = tick - 4
        if 0 <= i < QUARTERED:
            remote(
                xbuf.at[i, part(across)], xbuf.at[i, part(across)], fs.at[i], fr.at[i],
                {"tp": t_right},
            ).wait_recv()
            if i == 0:
                far_product()
            elif i % 2 == 0:
                pair_product(i // 2)
            if i == 2:
                for direction in range(2):
                    send_kv(1, direction, 1 - direction)
                    send_kv(1, direction, direction)
                for direction in range(2):
                    send_q(0, direction, direction)
                for direction in range(2):
                    send_q(1, direction, 1 - direction)
    for direction in range(2):
        for piece in range(2):
            send_kv(2, direction, piece)
    over_z[QUARTERED].wait_recv()
    over_z[QUARTERED + 1].wait_recv()
    pair_product(3)
    for direction in range(2):
        for piece in range(2):
            send_kv(3, direction, piece)
    for direction in range(2):
        send_q(1, direction, direction)

    def rotated(x):
        return x * rope[0] + pltpu.roll(x, HEAD // 2, 1) * rope[1]

    for piece in range(2):
        kv_copy(3, 0, piece).wait_recv()
        kv_copy(3, 1, piece).wait_recv()
        x = own[:, PIECE_COLS[piece]]
        x = x + kv_inbox[0, 3, piece].astype(F32)
        x = (x + kv_inbox[1, 3, piece].astype(F32)) * row_scale[...]
        if piece == 0:
            x = rotated(x)
        kv[:, piece * HEAD : (piece + 1) * HEAD] = x.astype(BF16)

    def z_of(i):
        return lax.rem(u + Z_STEPS[i] + NZ, NZ)

    def shard(owner, i):
        return kv_all.at[owner * NZ + z_of(i)]

    def held(i):
        return kv if i == 0 else shard(b, i)

    def z_copy(i, src, dst):
        to = u_right if Z_STEPS[i] < 0 else u_left
        return remote(src, dst, gzs.at[i], gzr.at[i], {"uly": to})

    def x_send(i, direction):
        return remote(
            held(i), shard(b, i), gxs.at[i, direction], gxr.at[i, direction],
            {"blk": b_right if direction == 0 else b_left},
        )

    def x_wait(i, direction):
        source = b_left if direction == 0 else b_right
        return remote(
            shard(source, i), shard(source, i), gxs.at[i, direction], gxr.at[i, direction],
            {"blk": b_right},
        )

    def x_pass(i):
        source, target = (b_left, b_right) if i % 2 == 0 else (b_right, b_left)
        return remote(shard(source, i), shard(source, i), gfs.at[i], gfr.at[i], {"blk": target})

    def side(i, m):
        owner = (b, b_left, b_right, b_across)[m]
        src = held(i) if m == 0 else shard(owner, i)
        return remote(src, shard(owner, i), gss.at[i, m], gsr.at[i, m], {"blk": sibling})

    def side_wait(i, m):
        owner = lax.rem(sibling + (0, 6, 2, 4)[m], 8)
        return remote(shard(owner, i), shard(owner, i), gss.at[i, m], gsr.at[i, m], {"blk": sibling})

    z_sends = []

    def start_z(step, src_i):
        copy = z_copy(Z_STEPS.index(step), held(src_i), shard(b, src_i))
        copy.start()
        z_sends.append(copy)

    place_own = pltpu.make_async_copy(kv, kv_all.at[b * NZ + u], lsem.at[2])

    def gather_tick(tick):
        i = tick
        if i < NZ:
            step = Z_STEPS[i]
            if i == 0:
                start_z(-1, 0)
                start_z(1, 0)
                place_own.start()
            else:
                z_copy(i, shard(b, i), shard(b, i)).wait_recv()
                if -4 < step < 0:
                    start_z(step - 1, i)
                if 0 < step < 3:
                    start_z(step + 1, i)
            x_send(i, 0).start()
            x_send(i, 1).start()
            side(i, 0).start()
        i = tick - 2
        if 0 <= i < NZ:
            x_wait(i, 0).wait_recv()
            x_wait(i, 1).wait_recv()
            x_pass(i).start()
            side(i, 1).start()
            side(i, 2).start()
        i = tick - 4
        if 0 <= i < NZ:
            remote(
                shard(b_across, i), shard(b_across, i), gfs.at[i], gfr.at[i], {"blk": b_right}
            ).wait_recv()
            side(i, 3).start()

    def finish_q(piece):
        q_copy(3, 0, piece).wait_recv()
        q_copy(3, 1, piece).wait_recv()
        cols = PIECE_COLS[2 + piece]
        x = own[:, cols] + q_inbox[0, 3, piece].astype(F32)
        own[:, cols] = (x + q_inbox[1, 3, piece].astype(F32)) * (row_scale[:, :1] * QSCALE)
        for h in range(piece * HEADS // 2, (piece + 1) * HEADS // 2):
            x = rotated(own[:, h * HEAD : (h + 1) * HEAD])
            q_out[h * ROWS : (h + 1) * ROWS, :] = x.astype(BF16)

    gather_tick(0)
    for direction in range(2):
        send_q(2, direction, 1 - direction)
    gather_tick(1)
    gather_tick(2)
    for direction in range(2):
        send_q(2, direction, direction)
    gather_tick(3)
    gather_tick(4)
    for direction in range(2):
        send_q(3, direction, 1 - direction)
    gather_tick(5)
    gather_tick(6)
    for direction in range(2):
        send_q(3, direction, direction)
    gather_tick(7)
    gather_tick(8)
    finish_q(0)
    gather_tick(9)
    finish_q(1)
    gather_tick(10)
    gather_tick(11)
    place_own.wait()
    for i in range(NZ):
        for m in range(4):
            side_wait(i, m).wait_recv()

    for copy in over_z:
        copy.wait_send()
    for i in range(QUARTERED):
        chunk_from(i, t, 0).wait_send()
        chunk_from(i, t, 1).wait_send()
        pass_on(i).wait_send()
    for direction in range(2):
        for step in range(4):
            for piece in range(2):
                if step > 0 or piece == direction:
                    kv_copy(step, direction, piece).wait_send()
                    q_copy(step, direction, piece).wait_send()
    for copy in z_sends:
        copy.wait_send()
    for i in range(NZ):
        x_send(i, 0).wait_send()
        x_send(i, 1).wait_send()
        x_pass(i).wait_send()
        for m in range(4):
            side(i, m).wait_send()


ANY = pl.BlockSpec(memory_space=pl.ANY)
VM = pl.BlockSpec(memory_space=pltpu.VMEM)
DMA = pltpu.SemaphoreType.DMA


HBM = pl.BlockSpec(memory_space=pltpu.HBM)
SM = pl.BlockSpec(memory_space=pltpu.SMEM)


def project(order, freq, gain, hidden, weights):
    n = NZ - 1
    return pl.pallas_call(
        proj_kernel,
        out_shape=(
            jax.ShapeDtypeStruct((HEADS * ROWS, HEAD), BF16),
            jax.ShapeDtypeStruct((8 * NZ, ROWS, 2 * HEAD), BF16),
        ),
        in_specs=[SM, VM, VM, HBM, HBM],
        out_specs=(VM, HBM),
        scratch_shapes=[
            pltpu.VMEM((ROWS, NZ * FEAT), BF16),
            pltpu.VMEM((FEAT, COLS), BF16),
            pltpu.VMEM((FEAT, COLS), BF16),
            pltpu.VMEM((NZ * FEAT // 128, 128), F32),
            pltpu.VMEM((n, ROWS, FEAT), BF16),
            pltpu.VMEM((ROWS, COLS), F32),
            pltpu.VMEM((ROWS, COLS), F32),
            pltpu.VMEM((3, 2 * ROWS, COLS), F32),
            pltpu.VMEM((ROWS, 2 * HEAD), BF16),
            pltpu.VMEM((2, ROWS, HEAD), F32),
            pltpu.VMEM((ROWS, HEAD), F32),
            pltpu.VMEM((2, 4, 2, ROWS, HEAD), BF16),
            pltpu.VMEM((2, 4, 2, ROWS, HEAD), BF16),
            pltpu.VMEM((2, 4, 2, ROWS, KCOL // 2), BF16),
            pltpu.VMEM((2, 4, 2, ROWS, KCOL // 2), BF16),
            DMA((3,)),
            DMA((n,)), DMA((n,)),
            DMA((n, 2)), DMA((n, 2)),
            DMA((n,)), DMA((n,)),
            DMA((2, 4, 2)), DMA((2, 4, 2)),
            DMA((2, 4, 2)), DMA((2, 4, 2)),
            DMA((NZ,)), DMA((NZ,)),
            DMA((NZ, 2)), DMA((NZ, 2)),
            DMA((NZ,)), DMA((NZ,)),
            DMA((NZ, 4)), DMA((NZ, 4)),
        ],
        compiler_params=pltpu.CompilerParams(
            collective_id=0, has_side_effects=True, vmem_limit_bytes=62 << 20
        ),
        name="project",
    )(order, freq, gain, hidden, weights)


def attend_kernel(order, docs, q, kv, out, inverse, m_ref, l_ref, acc):
    per = BLOCK // ROWS
    shard = lax.axis_index("blk") * NZ + lax.axis_index("uly")
    q_block = order[shard // per] * per + lax.rem(shard, per)
    for r in range(16):
        inverse[order[r]] = r
    segment = docs[pl.ds(q_block, 1), :]
    starts = jnp.zeros((1, ROWS), jnp.int32)
    for n in range(1, 16):
        before = jnp.sum((docs[...] < n).astype(jnp.int32))
        starts = jnp.where(segment == n, before, starts)
    count = q_block - jnp.min(starts) // ROWS + 1
    wide = HEADS * ROWS
    m_ref[...] = jnp.full((1, wide), NEG_BIG, F32)
    l_ref[...] = jnp.zeros((1, wide), F32)
    acc[...] = jnp.zeros((HEAD, wide), F32)
    lane = lax.broadcasted_iota(jnp.int32, (128, ROWS), 1)
    row = lax.broadcasted_iota(jnp.int32, (128, ROWS), 0)
    causal = row <= lane
    starts = jnp.broadcast_to(starts, (128, ROWS))

    def place(k_block):
        k_block = jnp.maximum(k_block, 0)
        return inverse[k_block // per] * per + lax.rem(k_block, per)

    def scores_of(i):
        k_block = q_block - i
        scores = lax.dot_general(
            kv[place(k_block), :, :HEAD], q[...], (((1,), (1,)), ((), ())), preferred_element_type=F32
        )
        allowed = (row + k_block * 128 >= starts) & (causal | (i > 0))
        bias = jnp.where(allowed, 0.0, NEG_BIG)
        return scores + jnp.concatenate([bias] * HEADS, axis=1)

    def mix(i, weights):
        return lax.dot_general(
            kv[place(q_block - i), :, HEAD:], weights.astype(BF16), (((0,), (0,)), ((), ())),
            preferred_element_type=F32,
        )

    def step(j, carry):
        near, past = scores_of(2 * j), scores_of(2 * j + 1)
        m_old = m_ref[...]
        m_new = jnp.maximum(m_old, jnp.max(jnp.maximum(near, past), axis=0, keepdims=True))
        near, past = jnp.exp2(near - m_new), jnp.exp2(past - m_new)
        factor = jnp.exp2(m_old - m_new)
        m_ref[...] = m_new
        l_ref[...] = l_ref[...] * factor + jnp.sum(near + past, axis=0, keepdims=True)
        acc[...] = acc[...] * factor + (mix(2 * j, near) + mix(2 * j + 1, past))
        return carry

    lax.fori_loop(0, (count + 1) // 2, step, 0)
    result = acc[...] / l_ref[...]
    for h in range(HEADS):
        part = result[:, h * ROWS : (h + 1) * ROWS]
        out[:, h * HEAD : (h + 1) * HEAD] = part.T.astype(BF16)


def attend(order, docs, q, kv):
    wide = HEADS * ROWS
    return pl.pallas_call(
        attend_kernel,
        out_shape=jax.ShapeDtypeStruct((ROWS, HEADS * HEAD), BF16),
        in_specs=[SM, VM, VM, VM],
        out_specs=VM,
        scratch_shapes=[
            pltpu.SMEM((16,), jnp.int32),
            pltpu.VMEM((1, wide), F32),
            pltpu.VMEM((1, wide), F32),
            pltpu.VMEM((HEAD, wide), F32),
        ],
        compiler_params=pltpu.CompilerParams(vmem_limit_bytes=60 << 20),
        name="attend",
    )(order, docs, q, kv)


PIECES = 4
HOPS = 4
PROWS = ROWS // PIECES
OUTW = 1024


def out_kernel(att, w, out, wloc, abuf, far_stage, near_stage, far_box, near_box,
               lsem, zs, zr, fs, fr, ns, nr):
    u = lax.axis_index("uly")
    t = lax.axis_index("tp")
    t_right, t_left = lax.rem(t + 1, NT), lax.rem(t + NT - 1, NT)
    u_right, u_left = lax.rem(u + 1, NZ), lax.rem(u + NZ - 1, NZ)
    load_w = pltpu.make_async_copy(w, wloc, lsem.at[0])
    load_w.start()
    own_copies = []
    for p in range(PIECES):
        copy = pltpu.make_async_copy(att.at[p], abuf.at[u, p], lsem.at[1 + p])
        copy.start()
        own_copies.append(copy)
    greet([{"uly": u_right}, {"uly": u_left}, {"tp": t_right}, {"tp": t_left}])

    def z_hops(p, direction):
        return 4 if (p + direction) % 2 == 0 else 3

    def chunk(direction, h):
        return lax.rem(u + NZ + (-h if direction == 0 else h), NZ)

    def z_copy(p, direction, h, source):
        src = att.at[p] if h == 0 else abuf.at[source, p]
        return remote(
            src, abuf.at[source, p], zs.at[p, direction, h], zr.at[p, direction, h],
            {"uly": u_right if direction == 0 else u_left},
        )

    def z_send(p, direction, h):
        return z_copy(p, direction, h, chunk(direction, h))

    def z_wait(p, direction, h):
        source = chunk(direction, h + 1)
        return remote(
            abuf.at[source, p], abuf.at[source, p], zs.at[p, direction, h],
            zr.at[p, direction, h], {"uly": u_right},
        )

    def z_step(p, h):
        for direction in range(2):
            hops = z_hops(p, direction)
            if h > 0 and h <= hops:
                z_wait(p, direction, h - 1).wait_recv()
            if h < hops:
                z_send(p, direction, h).start()

    def product(p, rel):
        d = lax.rem(t + rel, NT)
        x = abuf[pl.ds(2 * d, 2), p].reshape(2 * PROWS, FEAT)
        return dot32(x, wloc[...])

    def half(side):
        return slice(side * (OUTW // 2), (side + 1) * (OUTW // 2))

    def far_send(p, side):
        return remote(
            far_stage.at[p, side], far_box.at[p, side], fs.at[p, side], fr.at[p, side],
            {"tp": t_right if side == 0 else t_left},
        )

    def near_send(p, direction, side):
        return remote(
            near_stage.at[p, direction, side], near_box.at[p, direction, side],
            ns.at[p, direction, side], nr.at[p, direction, side],
            {"tp": t_right if direction == 0 else t_left},
        )

    def finish(p):
        mine = sides[p]
        for side in range(2):
            near_send(p, 0, side).wait_recv()
            near_send(p, 1, side).wait_recv()
            summed = mine[:, half(side)] + near_box[p, 0, side].astype(F32)
            summed = summed + near_box[p, 1, side].astype(F32)
            out[:, p, :, half(side)] = summed.reshape(2, PROWS, OUTW // 2).astype(BF16)

    z_step(0, 0)
    load_w.wait()
    for copy in own_copies:
        copy.wait()
    sides = {}
    for slot in range(1, PIECES + HOPS + 2):
        for p in range(PIECES):
            if 0 <= slot - p <= HOPS:
                z_step(p, slot - p)
        p = slot - HOPS
        if 0 <= p < PIECES:
            value = product(p, 2)
            for side in range(2):
                far_stage[p, side] = value[:, half(side)].astype(BF16)
                far_send(p, side).start()
            right = product(p, 1)
            near_stage[p, 0, 1] = right[:, half(1)].astype(BF16)
            near_send(p, 0, 1).start()
            left = product(p, 3)
            near_stage[p, 1, 0] = left[:, half(0)].astype(BF16)
            near_send(p, 1, 0).start()
            sides[p] = right[:, half(0)], left[:, half(1)]
        p = slot - HOPS - 1
        if 0 <= p < PIECES:
            right, left = sides[p]
            far_send(p, 0).wait_recv()
            near_stage[p, 0, 0] = (right + far_box[p, 0].astype(F32)).astype(BF16)
            near_send(p, 0, 0).start()
            far_send(p, 1).wait_recv()
            near_stage[p, 1, 1] = (left + far_box[p, 1].astype(F32)).astype(BF16)
            near_send(p, 1, 1).start()
            mine = product(p, 0)
            sides[p] = mine
        p = slot - HOPS - 2
        if 0 <= p < PIECES:
            finish(p)
    for p in range(PIECES):
        for direction in range(2):
            for h in range(z_hops(p, direction)):
                z_send(p, direction, h).wait_send()
            far_send(p, direction).wait_send()
            for side in range(2):
                near_send(p, direction, side).wait_send()


def project_out(attended, w):
    half = OUTW // 2
    out = pl.pallas_call(
        out_kernel,
        out_shape=jax.ShapeDtypeStruct((2, PIECES, PROWS, OUTW), BF16),
        in_specs=[ANY, HBM],
        out_specs=VM,
        scratch_shapes=[
            pltpu.VMEM((FEAT, OUTW), BF16),
            pltpu.VMEM((NZ, PIECES, PROWS, FEAT), BF16),
            pltpu.VMEM((PIECES, 2, 2 * PROWS, half), BF16),
            pltpu.VMEM((PIECES, 2, 2, 2 * PROWS, half), BF16),
            pltpu.VMEM((PIECES, 2, 2 * PROWS, half), BF16),
            pltpu.VMEM((PIECES, 2, 2, 2 * PROWS, half), BF16),
            DMA((1 + PIECES,)),
            DMA((PIECES, 2, 4)), DMA((PIECES, 2, 4)),
            DMA((PIECES, 2)), DMA((PIECES, 2)),
            DMA((PIECES, 2, 2)), DMA((PIECES, 2, 2)),
        ],
        compiler_params=pltpu.CompilerParams(
            collective_id=2, has_side_effects=True, vmem_limit_bytes=62 << 20
        ),
        name="project_out",
    )(attended.reshape(PIECES, PROWS, FEAT), w)
    return out.reshape(2 * ROWS, OUTW)


def rope_frequencies():
    base = THETA ** (-2.0 * np.arange(HEAD // 2, dtype=np.float64) / HEAD)
    wavelen = 2.0 * np.pi / base
    smooth = (8192.0 / wavelen - 1.0) / 3.0
    blended = (1.0 - smooth) * base / 8.0 + smooth * base
    scaled = np.where(wavelen > 8192.0, base / 8.0, np.where(wavelen < 2048.0, base, blended))
    return jnp.asarray(np.tile(scaled, 2)[None, :], F32)


def on_device(hidden, norm_gain, query_key_value_weight, w_out, doc_ids, block_order):
    weights = query_key_value_weight.reshape(FEAT, COLS)
    gain = norm_gain.reshape(NZ * FEAT // 128, 128)
    docs = doc_ids.reshape(NZ * FEAT // 128, 128)
    q, kv_all = project(block_order, rope_frequencies(), gain, hidden, weights)
    attended = attend(block_order, docs, q, kv_all)
    return project_out(attended, w_out)


def solution(mesh):
    return jax.shard_map(
        on_device,
        mesh=mesh,
        in_specs=(P(("blk", "uly"), None), P(), P("uly", "tp", None), P("tp", "uly"), P(), P()),
        out_specs=P(("blk", "tp"), "uly"),
        check_vma=False,
    )
```
